32 devices in a mesh: row: 4 (over y, core), col: 8 (over z, x).
Axes of the slice: x: 2, y: 2, z: 4, core: 2. Of those that a mesh axis runs over, the one named last changes fastest.
Arguments:
- front: float32 [12288, 12288], P('row', 'col'), may hold values from -6 to 6
- delayed: float32 [64, 12288], P('col', 'row'), may hold values from -6 to 6
- dest: int32 [64], P('col'), may hold values from 0 to 1023, as said below
- pivots: int32 [1024], replicated, may hold values from 0 to 12287, as said below
- pair_flags: int32 [1024], replicated, may hold values from 0 to 1, as said below
- linv: float32 [4, 256, 256], replicated, as said below
- dinv_diag: float32 [1024], replicated, may hold values from -0.1 to 0.1
- dinv_off: float32 [1024], replicated, may hold values from -0.08 to 0.08
Outputs:
- trailing: float32 [12288, 12288], P('row', 'col')
- factor: float32 [12288, 1024], P('row')
The draws below stay inside these ranges and needn't reach their ends.
Inputs may be any that keep to these rules, and one draw needn't show every extreme that they name: Distinct front columns; slots p * 256 to (p + 1) * 256 - 1 are panel p's pivots. Each block of 1536 columns held by one index of col contains exactly 128 of them. `pair_flags`: A 1 at slot s joins slots s and s + 1 into one 2x2 block; no two 1s are adjacent and the last slot of a panel holds 0. `dest`: several delayed columns may share a slot. Of the 8 delayed columns held by one index of col, at most 2 go to pivot columns held by the same index of col. `linv`: each panel's matrix is unit lower triangular: ones on the diagonal, zeros above it.
All inputs are finite; a program needn't handle non-finite values.
Results may differ from the reference program's by a relative error of at most 0.00015.
Values sent between devices are 32-bit elements; how exact they have to be, the bound alone decides.
A program may use at most 192 MiB of HBM per device.

```python
import jax
import jax.numpy as jnp
from jax import lax

NF = 12288
PANEL = 256
PANELS = 4
DEL_COL = 8
CAP = 2
CB = 1536
E = 1024
PIV_OWN = 128
NDEL = 64
N_COL = 8


def pivot_layout(key):
    base = jax.random.fold_in(key, 7)
    picks = jax.vmap(lambda owner: jax.random.permutation(jax.random.fold_in(base, owner), CB)[:PIV_OWN].astype(jnp.int32) + owner * CB)(jnp.arange(N_COL, dtype=jnp.int32))
    listed = picks.reshape(-1).astype(jnp.int32)
    order = jax.random.permutation(jax.random.fold_in(key, 11), E).astype(jnp.int32)
    placed = jnp.zeros((E,), jnp.int32).at[order].set(listed)
    return (placed, order.reshape(N_COL, PIV_OWN))


def draw_pivots(key, part):
    return pivot_layout(key)[0]


def draw_dest(key, part):
    placed, slot_table = pivot_layout(key)
    inner = jax.random.fold_in(key, 23)
    heavy = jax.random.randint(jax.random.fold_in(inner, 1), (), 0, N_COL).astype(jnp.int32)
    shifts = jax.random.randint(jax.random.fold_in(inner, 2), (N_COL,), 0, N_COL - 1).astype(jnp.int32)
    position = jnp.arange(DEL_COL, dtype=jnp.int32)
    others = (heavy + 1 + (shifts[:, None] + position[None, :] - CAP) % (N_COL - 1)) % N_COL
    owners = jnp.where(position[None, :] < CAP, heavy, others)
    choose = jax.random.randint(jax.random.fold_in(inner, 3), (N_COL, DEL_COL), 0, PIV_OWN).astype(jnp.int32)
    return slot_table[owners, choose].reshape(-1).astype(jnp.int32)


def draw_pair_flags(key, part):
    wanted = jax.random.randint(key, (E,), 0, 5) < 2
    closing = jnp.arange(E) % PANEL == PANEL - 1

    def advance(previous, inputs):
        want_here, close_here = inputs
        result = jnp.where(want_here & (previous == 0) & jnp.logical_not(close_here), 1, 0).astype(jnp.int32)
        return (result, result)
    _, flags_out = lax.scan(advance, jnp.int32(0), (wanted, closing))
    return flags_out


def draw_linv(key, part):
    values = 0.05 * jax.random.normal(key, (PANELS, PANEL, PANEL), jnp.float32)
    lower = jnp.arange(PANEL)[:, None] > jnp.arange(PANEL)[None, :]
    return jnp.where(lower[None], values, 0.0) + jnp.eye(PANEL, dtype=jnp.float32)[None]


def steps_of(rng, shape, pieces, smallest, top_value):
    def one(dim, shards_of):
        steps = jax.random.uniform(jax.random.fold_in(jax.random.fold_in(rng, 6), dim), (shards_of,), jnp.float32, smallest / len(pieces), top_value / len(pieces))
        return jnp.repeat(jnp.exp(steps), shape[dim] // shards_of).reshape((-1,) + (1,) * (len(shape) - dim - 1))

    level = one(*pieces[0])
    for cut in pieces[1:]:
        level = level * one(*cut)
    return level


def noise(key, shape, deviation, reach, cuts=(), held_as=jnp.bfloat16):
    gain = steps_of(key, shape, cuts, -0.22, 0.18) if cuts else 1.0
    values = jax.random.normal(key, shape, jnp.float32) * deviation * gain
    return jnp.minimum(jnp.maximum(values, -reach), reach).astype(held_as)


def setup_inputs(seed: int = 0) -> dict:
    streams_of = jax.random.split(jax.random.key(seed), 9)
    front = noise(streams_of[0], (NF, NF), 1.0, 6.0, ((0, 4), (1, 8)), jnp.float32)
    delayed = noise(streams_of[1], (NDEL, NF), 1.0, 6.0, ((0, 8), (1, 4)), jnp.float32)
    dest = draw_dest(jax.random.fold_in(streams_of[8], 71), 0)
    pivots = draw_pivots(jax.random.fold_in(streams_of[8], 71), 0)
    pair_flags = draw_pair_flags(jax.random.fold_in(streams_of[8], 71), 0)
    linv = draw_linv(jax.random.fold_in(streams_of[8], 71), 0)
    dinv_diag = jnp.clip(jax.random.uniform(streams_of[6], (E,), jnp.float32, -0.1, 0.1), -0.1, 0.1)
    dinv_off = jnp.clip(jax.random.uniform(streams_of[7], (E,), jnp.float32, -0.08, 0.08), -0.08, 0.08)
    return {"front": front, "delayed": delayed, "dest": dest, "pivots": pivots, "pair_flags": pair_flags, "linv": linv, "dinv_diag": dinv_diag, "dinv_off": dinv_off}


precise = lax.Precision.HIGHEST


def pair_scale(scaled, pair_bits, diag_part, off_part):
    coupled = pair_bits.astype(jnp.float32) * off_part
    zero_col = jnp.zeros_like(scaled[:, :1])
    shifted_next = jnp.concatenate([scaled[:, 1:], zero_col], axis=1)
    shifted_prev = jnp.concatenate([zero_col, scaled[:, :-1]], axis=1)
    coupled_prev = jnp.concatenate([jnp.zeros_like(coupled[:1]), coupled[:-1]])
    return scaled * diag_part + shifted_next * coupled + shifted_prev * coupled_prev


def reference(front, delayed, dest, pivots, pair_flags, linv, dinv_diag, dinv_off):
    targets = pivots[dest]
    current = front.at[:, targets].add(jnp.transpose(delayed))
    factors = []
    for panel_index in range(PANELS):
        offset = panel_index * PANEL
        chosen = pivots[offset:offset + PANEL]
        panel_cols = current[:, chosen]
        scaled = jnp.dot(panel_cols, jnp.transpose(linv[panel_index]), precision=precise)
        columns = pair_scale(scaled, pair_flags[offset:offset + PANEL], dinv_diag[offset:offset + PANEL], dinv_off[offset:offset + PANEL])
        current = current - jnp.dot(columns, jnp.transpose(scaled), precision=precise)
        factors.append(columns)
    retained = jnp.ones((NF,), jnp.float32).at[pivots].set(0.0)
    trailing = current * retained[:, None] * retained[None, :]
    return trailing, jnp.concatenate(factors, axis=1)
```

```python
import functools

import jax
import jax.numpy as jnp
from jax import lax
from jax.experimental import pallas as pl
from jax.experimental.pallas import tpu as pltpu
from jax.sharding import PartitionSpec as P

MESH = pl.DeviceIdType.MESH
VMEM_LIMIT = 62 * 1024 * 1024
F32 = jnp.float32
BF16 = jnp.bfloat16
CHUNK = 256
LANES = 128


def split(a):
    hi = a.astype(BF16)
    return hi, (a - hi.astype(F32)).astype(BF16)


def mm(a, b):
    return lax.dot_general(a, b, (((1,), (0,)), ((), ())), preferred_element_type=F32)


def mm_t(a, b):
    return lax.dot_general(a, b, (((1,), (1,)), ((), ())), preferred_element_type=F32)


def iota(shape, dim):
    return lax.broadcasted_iota(jnp.int32, shape, dim)


def one_hot(mask):
    return jnp.where(mask, 1.0, 0.0).astype(BF16)


def pick_kernel(front_ref, delayed_ref, dest_ref, irow_ref, icol_ref, raw_ref, piv_ref, g_ref, rowsel_ref, acc_ref, dacc_ref):
    i = pl.program_id(0)
    slots = irow_ref.shape[1]
    cols, wide = g_ref.shape
    per_row = rowsel_ref.shape[0]
    nd = delayed_ref.shape[0]
    ch = front_ref.shape[0]

    @pl.when(i == 0)
    def _():
        y = one_hot(icol_ref[:, 1:2] == iota((slots, wide), 1))

        @pl.loop(0, cols // CHUNK)
        def _(t):
            part = pl.ds(pl.multiple_of(t * CHUNK, CHUNK), CHUNK)
            x = one_hot(irow_ref[0:1, :] == iota((CHUNK, slots), 0) + t * CHUNK)
            g_ref[part, :] = mm(x, y).astype(BF16)

        rowsel_ref[...] = one_hot(irow_ref[1:2, :] == iota((per_row, slots), 0))
        acc_ref[...] = jnp.zeros_like(acc_ref)
        dacc_ref[...] = jnp.zeros_like(dacc_ref)

    hi, lo = split(front_ref[...])
    g = g_ref[...]
    raw = mm(hi, g) + mm(lo, g)
    raw_ref[0, :ch, :] = raw
    for b in range(ch // LANES):
        raw_ref[0, ch + b * nd : ch + (b + 1) * nd, :] = delayed_ref[:, b * LANES : (b + 1) * LANES]

    here = one_hot(icol_ref[:, 0:1] == iota((slots, ch), 1) + i * ch)
    sel = mm(rowsel_ref[...], here).astype(BF16)
    rh, rl = split(raw)
    acc_ref[...] += mm(sel, rh) + mm(sel, rl)
    dh, dl = split(delayed_ref[...])
    dacc_ref[...] += mm_t(dh, sel) + mm_t(dl, sel)

    @pl.when(i == pl.num_programs(0) - 1)
    def _():
        piv_ref[:per_row, :] = acc_ref[...]
        for b in range(per_row // LANES):
            piv_ref[per_row + b * nd : per_row + (b + 1) * nd, :] = dacc_ref[:, b * LANES : (b + 1) * LANES]
        piv_ref[per_row + per_row // LANES * nd :, :] = dest_ref[...]


def pick_columns(front, delayed, dest, irow, icol, wide, per_row):
    rows, cols = front.shape
    nd = delayed.shape[0]
    slots = irow.shape[1]
    n = rows // CHUNK
    high = CHUNK + nd * (CHUNK // LANES)
    piv_high = per_row + nd * (per_row // LANES) + nd
    return pl.pallas_call(
        pick_kernel,
        grid=(n,),
        in_specs=[
            pl.BlockSpec((CHUNK, cols), lambda i: (i, 0)),
            pl.BlockSpec((nd, CHUNK), lambda i: (0, i)),
            pl.BlockSpec((nd, wide), lambda i: (0, 0)),
            pl.BlockSpec((8, slots), lambda i: (0, 0)),
            pl.BlockSpec((slots, 8), lambda i: (0, 0)),
        ],
        out_specs=(
            pl.BlockSpec((1, high, wide), lambda i: (i, 0, 0)),
            pl.BlockSpec((piv_high, wide), lambda i: (0, 0)),
        ),
        out_shape=(
            jax.ShapeDtypeStruct((n, high, wide), F32),
            jax.ShapeDtypeStruct((piv_high, wide), F32),
        ),
        scratch_shapes=[
            pltpu.VMEM((cols, wide), BF16),
            pltpu.VMEM((per_row, slots), BF16),
            pltpu.VMEM((per_row, wide), F32),
            pltpu.VMEM((nd, per_row), F32),
        ],
        compiler_params=pltpu.CompilerParams(dimension_semantics=("arbitrary",), vmem_limit_bytes=VMEM_LIMIT),
    )(front, delayed, dest, irow, icol)


def gather_kernel(
    dims, raw_own, piv_own, linv_ref, coef_ref, irow_ref, icol_ref,
    cols_out, hi_out, lo_out,
    raw_all, col_raw, piv_all, rowperm, t1h, t1l, qh, ql, nh, nl, rd, mh, ml, stage, stage_h, stage_l,
    keep_sem, root_sem, raw_recv, raw_send, col_recv, col_send, piv_recv, piv_send, out_sem, hi_sem, lo_sem,
):
    zs, xs, ys, halves, per_row, nd, x_first = dims
    nc, n_row = zs * xs, ys * 2
    nch = raw_own.shape[0]
    high = raw_own.shape[1]
    hch = nch // halves
    panels, width, _ = linv_ref.shape
    slots = panels * width
    wide = raw_own.shape[2]
    ch = CHUNK
    kraw = nc * wide
    kall = mh.shape[0]
    row, col = lax.axis_index("row"), lax.axis_index("col")
    y, k = row // 2, row % 2
    z, x = col // xs, col % xs
    root = col // halves
    half = col % halves
    root_y, root_k = root // 2, root % 2
    is_root = row == root
    at_root_core = k == root_k
    reach = zs + xs - 2
    span = reach + ys - 1

    def at(y_, k_, z_, x_):
        return (y_ * 2 + k_, z_ * xs + x_)

    links = [
        (z + 1 < zs, at(y, k, z + 1, x)),
        (z >= 1, at(y, k, z - 1, x)),
        (x + 1 < xs, at(y, k, z, x + 1)),
        (x >= 1, at(y, k, z, x - 1)),
        (y + 1 < ys, at(y + 1, k, z, x)),
        (y >= 1, at(y - 1, k, z, x)),
        (None, at(y, 1 - k, z, x)),
    ]

    barrier = pltpu.get_barrier_semaphore()
    peers = 1
    for cond, dev in links:
        if cond is None:
            pl.semaphore_signal(barrier, inc=1, device_id=dev, device_id_type=MESH)
        else:
            peers = peers + jnp.where(cond, 1, 0)

            @pl.when(cond)
            def _(dev=dev):
                pl.semaphore_signal(barrier, inc=1, device_id=dev, device_id_type=MESH)
    pl.semaphore_wait(barrier, peers)

    def remote(way, src, dst, send, recv):
        return pltpu.make_async_remote_copy(
            src_ref=src, dst_ref=dst, send_sem=send, recv_sem=recv, device_id=links[way][1], device_id_type=MESH)

    def piv_ways(sy, c):
        zc, xc = c // xs, c % xs
        same_y = sy == y
        same_x = xc == x
        return [
            (0, (z + 1 < zs) & (zc <= z) & same_x & same_y),
            (1, (z >= 1) & (zc >= z) & same_x & same_y),
            (2, (x + 1 < xs) & (xc <= x) & same_y),
            (3, (x >= 1) & (xc >= x) & same_y),
            (4, (y + 1 < ys) & (sy <= y)),
            (5, (y >= 1) & (sy >= y)),
        ]

    def piv_copy(way, sy, c, src):
        s = sy * 2 + k
        return remote(way, src, piv_all.at[s, c], piv_send.at[way, sy * nc + c], piv_recv.at[s, c])

    def piv_arrived(s, c):
        pltpu.make_async_copy(piv_all.at[s, c], piv_all.at[s, c], piv_recv.at[s, c]).wait()

    def piv_step(sy, c, src):
        for way, cond in piv_ways(sy, c):
            @pl.when(cond)
            def _(way=way):
                piv_copy(way, sy, c, src).start()
        piv_copy(6, sy, c, src).start()

    def raw_ways(c, first):
        zc, xc = c // xs, c % xs
        same_x, same_z = xc == x, zc == z
        along_z = same_x | first
        along_x = same_z | jnp.logical_not(first)
        return [
            (0, (z + 1 < zs) & (zc <= z) & along_z),
            (1, (z >= 1) & (zc >= z) & along_z),
            (2, (x + 1 < xs) & (xc <= x) & along_x),
            (3, (x >= 1) & (xc >= x) & along_x),
        ]

    def col_copy(way, c, j, src):
        return remote(way, src, col_raw.at[c, j], col_send.at[way - 4, c], col_recv.at[c, j])

    def raw_step(c, i, src):
        for way, cond in raw_ways(c, i < x_first):
            @pl.when(cond)
            def _(way=way):
                remote(way, src, raw_all.at[c, i], raw_send.at[way, c], raw_recv.at[c, i]).start()
        j = i - half * hch

        @pl.when(is_root & (j >= 0) & (j < hch))
        def _():
            @pl.when(y + 1 < ys)
            def _():
                col_copy(4, c, j, src).start()

            @pl.when(y >= 1)
            def _():
                col_copy(5, c, j, src).start()
            col_copy(6, c, j, src).start()
            pltpu.make_async_copy(src, col_raw.at[c, j], root_sem.at[c, j]).start()

    def col_arrived(c, j):
        pltpu.make_async_copy(col_raw.at[c, j], col_raw.at[c, j], col_recv.at[c, j]).wait()

    keep_raw = pltpu.make_async_copy(raw_own, raw_all.at[col], keep_sem.at[0])
    keep_piv = pltpu.make_async_copy(piv_own, piv_all.at[row, col], keep_sem.at[1])
    keep_raw.start()
    keep_piv.start()

    def own_step(i):
        @pl.when(i < nch)
        def _():
            raw_step(col, i, raw_own.at[i])

    piv_step(y, col, piv_own)
    own_step(0)
    ahead = 1

    @pl.loop(1, span + 1)
    def _(s):
        @pl.loop(0, ys * nc)
        def _(q):
            sy, c = q // nc, q % nc
            dist = jnp.abs(c // xs - z) + jnp.abs(c % xs - x) + jnp.abs(sy - y)

            @pl.when(dist == s)
            def _():
                piv_arrived(sy * 2 + k, c)
                piv_step(sy, c, piv_all.at[sy * 2 + k, c])
        own_step(s)
    ahead = span + 1

    def panel(p, n=1):
        return slice(p * width, (p + n) * width)

    def gather_square():
        @pl.loop(0, ys * nc)
        def _(q):
            piv_arrived((q // nc) * 2 + 1 - k, q % nc)
        keep_piv.wait()

        @pl.loop(0, panels - 1)
        def _(p):
            part = pl.ds(pl.multiple_of(p * width, width), width)
            later = pl.ds(pl.multiple_of((p + 1) * width, width), width)
            rowperm[part, :] = one_hot(icol_ref[later, 2:3] == iota((width, n_row * per_row), 1))

        @pl.loop(0, nc // 2)
        def _(c2):
            block = jnp.concatenate(
                [
                    jnp.concatenate([piv_all[r, c2 * 2 + b, :per_row, :] for b in range(2)], axis=1)
                    for r in range(n_row)
                ],
                axis=0,
            )
            h, l = split(block)
            at_cols = pl.ds(pl.multiple_of(c2 * 2 * wide, 2 * wide), 2 * wide)

            @pl.loop(0, panels - 1)
            def _(p):
                part = pl.ds(pl.multiple_of(p * width, width), width)
                perm = rowperm[part, :]
                a, b = split(mm(perm, h) + mm(perm, l))
                t1h[part, at_cols] = a
                t1l[part, at_cols] = b
        rest = [
            jnp.concatenate(
                [
                    piv_all[r, c, per_row + b * nd : per_row + (b + 1) * nd, :]
                    for r in range(n_row)
                    for b in range(per_row // LANES)
                ],
                axis=1,
            )
            for c in range(nc)
        ]
        h, l = split(jnp.concatenate(rest, axis=0))

        @pl.loop(0, panels - 1)
        def _(p):
            part = pl.ds(pl.multiple_of(p * width, width), width)
            perm = rowperm[part, :]
            a, b = split(mm_t(perm, h) + mm_t(perm, l))
            t1h[part, kraw:] = a
            t1l[part, kraw:] = b

    def dests():
        return jnp.concatenate(
            [piv_all[0, c, per_row + per_row // LANES * nd :, 0:1] for c in range(nc)], axis=0
        ).astype(jnp.int32)

    def square():
        d = dests()

        @pl.loop(0, panels - 1)
        def _(p):
            part = pl.ds(pl.multiple_of(p * width, width), width)
            slot = irow_ref[2:3, part]
            take = one_hot(slot == iota((kraw, width), 0))
            put = one_hot(d == iota((nc * nd, width), 1) + p * width)
            take = jnp.concatenate([take, put], axis=0)

            @pl.loop(0, panels - 1)
            def _(r):
                rows = pl.ds(pl.multiple_of(r * width, width), width)
                h, l = split(mm(t1h[rows, :], take) + mm(t1l[rows, :], take))
                qh[rows, part] = h
                ql[rows, part] = l

    def dot3(a, b, f):
        return f(a[0], b[0]) + f(a[0], b[1]) + f(a[1], b[0])

    def recur():
        nh[...] = jnp.zeros_like(nh)
        nl[...] = jnp.zeros_like(nl)
        for p in range(panels):
            mine = split(linv_ref[p])
            nh[panel(p), panel(p)], nl[panel(p), panel(p)] = mine
            if p == 0:
                continue
            e, until = p - 1, slice(0, p * width)
            for q in range(p, panels):
                rows = panel(q - 1)
                r = dot3((qh[rows, until], ql[rows, until]), (nh[panel(e), until], nl[panel(e), until]), mm_t)
                rd[rows, panel(e)] = pair_scale(r, coef_ref, panel(e))
            b = dot3(mine, split(rd[panel(p - 1), until]), mm)
            out = dot3(split(-b), (nh[until, until], nl[until, until]), mm)
            nh[panel(p), until], nl[panel(p), until] = split(out)

    def spread():
        step = 2 * wide

        @pl.loop(0, kraw // step)
        def _(t):
            part = pl.ds(pl.multiple_of(t * step, step), step)
            take = one_hot(irow_ref[2:3, :] == iota((step, slots), 0) + t * step)
            mh[part, :] = mm_t(take, nh[...]).astype(BF16)
            ml[part, :] = mm_t(take, nl[...]).astype(BF16)
        put = one_hot(dests() == iota((nc * nd, slots), 1))
        mh[kraw:, :] = mm_t(put, nh[...]).astype(BF16)
        ml[kraw:, :] = mm_t(put, nl[...]).astype(BF16)

    def chunk_parts(ref, i):
        a = jnp.concatenate([ref[c, i, :ch, :] for c in range(nc)], axis=1)
        d = jnp.concatenate(
            [
                jnp.concatenate([ref[c, i, ch + b * nd : ch + (b + 1) * nd, :] for b in range(ch // LANES)], axis=1)
                for c in range(nc)
            ],
            axis=0,
        )
        return split(jnp.concatenate([a, d.T], axis=1))

    def scaled_tile(parts, part):
        return mm(parts[0], mh[:, part]) + mm(parts[0], ml[:, part]) + mm(parts[1], mh[:, part])

    def cols_copy(i):
        rows = pl.ds(pl.multiple_of(i * ch, ch), ch)
        return pltpu.make_async_copy(stage.at[i % 2], cols_out.at[rows, :], out_sem.at[i % 2])

    def eliminate(i):
        @pl.when(i >= 2)
        def _():
            cols_copy(i - 2).wait()
        parts = chunk_parts(raw_all, i)

        @pl.loop(0, panels)
        def _(p):
            part = pl.ds(pl.multiple_of(p * width, width), width)
            stage[i % 2, :, part] = pair_scale(scaled_tile(parts, part), coef_ref, part)
        cols_copy(i).start()

    def side_copies(j):
        cols = pl.ds(pl.multiple_of(j * ch, ch), ch)
        return (
            pltpu.make_async_copy(stage_h.at[j % 2], hi_out.at[:, cols], hi_sem.at[j % 2]),
            pltpu.make_async_copy(stage_l.at[j % 2], lo_out.at[:, cols], lo_sem.at[j % 2]),
        )

    def eliminate_side(j):
        @pl.when(k != root_k)
        def _():
            @pl.loop(0, nc)
            def _(c):
                col_arrived(c, j)

        @pl.when(is_root)
        def _():
            @pl.loop(0, nc)
            def _(c):
                pltpu.make_async_copy(col_raw.at[c, j], col_raw.at[c, j], root_sem.at[c, j]).wait()

        @pl.when(j >= 2)
        def _():
            for copy in side_copies(j - 2):
                copy.wait()
        parts = chunk_parts(col_raw, j)

        @pl.loop(0, panels)
        def _(p):
            part = pl.ds(pl.multiple_of(p * width, width), width)
            stage_h[j % 2, part, :], stage_l[j % 2, part, :] = split(scaled_tile(parts, part).T)
        for copy in side_copies(j):
            copy.start()

    first = max(reach - 1, 3)
    side_lag = reach - 1 + ys
    work = [gather_square, square, recur]

    @pl.loop(0, nch + max(first, side_lag))
    def _(s):
        own_step(s + ahead)

        @pl.loop(0, nc)
        def _(c):
            dist = jnp.abs(c // xs - z) + jnp.abs(c % xs - x)
            i = s - (dist - 1)

            @pl.when((dist >= 1) & (i >= 0) & (i < nch))
            def _():
                pltpu.make_async_copy(raw_all.at[c, i], raw_all.at[c, i], raw_recv.at[c, i]).wait()
                raw_step(c, i, raw_all.at[c, i])

        @pl.when(at_root_core & (y != root_y))
        def _():
            @pl.loop(0, nc)
            def _(c):
                dist = jnp.abs(c // xs - z) + jnp.abs(c % xs - x)
                j = s - (jnp.maximum(dist, 1) - 1) - jnp.abs(y - root_y) - half * hch

                @pl.when((j >= 0) & (j < hch))
                def _():
                    col_arrived(c, j)
                    src = col_raw.at[c, j]

                    @pl.when((y > root_y) & (y + 1 < ys))
                    def _():
                        col_copy(4, c, j, src).start()

                    @pl.when((y < root_y) & (y >= 1))
                    def _():
                        col_copy(5, c, j, src).start()
                    col_copy(6, c, j, src).start()

        for n, piece in enumerate(work):
            pl.when(s == n)(piece)

        @pl.when(s == len(work) - 1)
        def _():
            spread()
            keep_raw.wait()

        i = s - first

        @pl.when((i >= 0) & (i < nch))
        def _():
            eliminate(i)
        j = s - side_lag - half * hch

        @pl.when((j >= 0) & (j < hch))
        def _():
            eliminate_side(j)

    for i in range(max(nch - 2, 0), nch):
        cols_copy(i).wait()
    for j in range(max(hch - 2, 0), hch):
        for copy in side_copies(j):
            copy.wait()

    @pl.loop(0, ys * nc)
    def _(q):
        sy, c = q // nc, q % nc
        for way, cond in piv_ways(sy, c):
            @pl.when(cond)
            def _(way=way):
                piv_copy(way, sy, c, piv_own).wait_send()
        piv_copy(6, sy, c, piv_own).wait_send()

    def sent(ref, sem):
        pltpu.make_async_copy(ref, ref, sem).wait()

    @pl.loop(0, nc)
    def _(c):
        for (way, late), (_, early) in zip(raw_ways(c, False), raw_ways(c, True)):
            sem = raw_send.at[way, c]

            @pl.when(late & early)
            def _(sem=sem):
                sent(raw_all.at[c], sem)

            if x_first:
                @pl.when(jnp.logical_not(late) & early)
                def _(sem=sem):
                    sent(raw_all.at[c, pl.ds(0, x_first)], sem)

                @pl.when(late & jnp.logical_not(early))
                def _(sem=sem):
                    sent(raw_all.at[c, pl.ds(x_first, nch - x_first)], sem)
            else:
                @pl.when(late & jnp.logical_not(early))
                def _(sem=sem):
                    sent(raw_all.at[c], sem)

        @pl.when(is_root | (at_root_core & (y > root_y)))
        def _():
            @pl.when(y + 1 < ys)
            def _():
                sent(col_raw.at[c], col_send.at[0, c])

        @pl.when(is_root | (at_root_core & (y < root_y)))
        def _():
            @pl.when(y >= 1)
            def _():
                sent(col_raw.at[c], col_send.at[1, c])

        @pl.when(at_root_core)
        def _():
            sent(col_raw.at[c], col_send.at[2, c])


def pair_scale(scaled, coef_ref, part):
    width = scaled.shape[1]
    return (
        scaled * coef_ref[0:1, part]
        + pltpu.roll(scaled, width - 1, 1) * coef_ref[1:2, part]
        + pltpu.roll(scaled, 1, 1) * coef_ref[2:3, part]
    )


def gather(raw, piv, linv, coef, irow, icol, cols, per_row, nd):
    n_col = lax.axis_size("col")
    n_row = lax.axis_size("row")
    nch, high, wide = raw.shape
    panels, width, _ = linv.shape
    slots = panels * width
    rows = nch * CHUNK
    halves = rows // cols
    ys = n_row // 2
    xs = ys if n_col % ys == 0 else 1
    zs = n_col // xs
    hch = nch // halves
    x_first = nch // 6
    kall = n_col * (wide + nd)
    early = slots - width
    vmem = pl.BlockSpec(memory_space=pltpu.VMEM)
    hbm = pl.BlockSpec(memory_space=pl.ANY)
    dma = pltpu.SemaphoreType.DMA
    return pl.pallas_call(
        functools.partial(gather_kernel, (zs, xs, ys, halves, per_row, nd, x_first)),
        out_shape=(
            jax.ShapeDtypeStruct((rows, slots), F32),
            jax.ShapeDtypeStruct((slots, cols), BF16),
            jax.ShapeDtypeStruct((slots, cols), BF16),
        ),
        in_specs=[vmem] * 6,
        out_specs=(hbm, hbm, hbm),
        scratch_shapes=[
            pltpu.VMEM((n_col, nch, high, wide), F32),
            pltpu.VMEM((n_col, hch, high, wide), F32),
            pltpu.VMEM((n_row, n_col) + piv.shape, F32),
            pltpu.VMEM((early, slots), BF16),
            pltpu.VMEM((early, kall), BF16),
            pltpu.VMEM((early, kall), BF16),
            pltpu.VMEM((early, early), BF16),
            pltpu.VMEM((early, early), BF16),
            pltpu.VMEM((slots, slots), BF16),
            pltpu.VMEM((slots, slots), BF16),
            pltpu.VMEM((early, early), F32),
            pltpu.VMEM((kall, slots), BF16),
            pltpu.VMEM((kall, slots), BF16),
            pltpu.VMEM((2, CHUNK, slots), F32),
            pltpu.VMEM((2, slots, CHUNK), BF16),
            pltpu.VMEM((2, slots, CHUNK), BF16),
            dma((2,)),
            dma((n_col, hch)),
            dma((n_col, nch)),
            dma((4, n_col)),
            dma((n_col, hch)),
            dma((3, n_col)),
            dma((n_row, n_col)),
            dma((7, ys * n_col)),
            dma((2,)),
            dma((2,)),
            dma((2,)),
        ],
        compiler_params=pltpu.CompilerParams(
            collective_id=0, has_side_effects=True, vmem_limit_bytes=VMEM_LIMIT
        ),
    )(raw, piv, linv, coef, irow, icol)


def trailing_kernel(tile, c_ref, hi_ref, lo_ref, front_ref, rkeep_ref, ckeep_ref, out_ref, factor_ref):
    cols = hi_ref.shape[1]
    columns = c_ref[...]
    factor_ref[...] = columns
    hi, lo = split(columns)
    rkeep = rkeep_ref[...] > 0.0

    @pl.loop(0, cols // tile)
    def _(i):
        part = pl.ds(pl.multiple_of(i * tile, tile), tile)
        bh, bl = hi_ref[:, part], lo_ref[:, part]
        acc = mm(hi, bh) + mm(hi, bl) + mm(lo, bh)
        out_ref[:, part] = jnp.where(rkeep & (ckeep_ref[:, part] > 0.0), front_ref[:, part] - acc, 0.0)


def update(columns, side_hi, side_lo, front, row_keep, col_keep):
    rows, cols = front.shape
    slots = columns.shape[1]
    tile = 256
    return pl.pallas_call(
        functools.partial(trailing_kernel, tile),
        grid=(rows // tile,),
        in_specs=[
            pl.BlockSpec((tile, slots), lambda i: (i, 0)),
            pl.BlockSpec((slots, cols), lambda i: (0, 0)),
            pl.BlockSpec((slots, cols), lambda i: (0, 0)),
            pl.BlockSpec((tile, cols), lambda i: (i, 0)),
            pl.BlockSpec((tile, 1), lambda i: (i, 0)),
            pl.BlockSpec((1, cols), lambda i: (0, 0)),
        ],
        out_specs=(
            pl.BlockSpec((tile, cols), lambda i: (i, 0)),
            pl.BlockSpec((tile, slots), lambda i: (i, 0)),
        ),
        out_shape=(
            jax.ShapeDtypeStruct((rows, cols), F32),
            jax.ShapeDtypeStruct((rows, slots), F32),
        ),
        compiler_params=pltpu.CompilerParams(dimension_semantics=("arbitrary",), vmem_limit_bytes=VMEM_LIMIT),
    )(columns, side_hi, side_lo, front, row_keep, col_keep)


def body(front, delayed, dest, pivots, pair_flags, linv, dinv_diag, dinv_off):
    n_col = lax.axis_size("col")
    n_row = lax.axis_size("row")
    rows, cols = front.shape
    row_id = lax.axis_index("row")
    col_id = lax.axis_index("col")
    row_start = row_id * rows
    col_start = col_id * cols
    panels, width, _ = linv.shape
    slots = pivots.shape[0]
    per_col = slots // n_col
    per_row = slots // n_row
    wide = (per_col + LANES - 1) // LANES * LANES
    nd = delayed.shape[0]
    slot_ids = jnp.arange(slots, dtype=jnp.int32)

    col_owner = pivots // cols
    row_owner = pivots // rows
    before = slot_ids[None, :] < slot_ids[:, None]
    col_rank = jnp.sum((before & (col_owner[:, None] == col_owner[None, :])).astype(jnp.int32), axis=1)
    row_rank = jnp.sum((before & (row_owner[:, None] == row_owner[None, :])).astype(jnp.int32), axis=1)
    col_pos = col_owner * wide + col_rank
    row_pos = row_owner * per_row + row_rank
    pad = jnp.zeros_like(pivots)
    irow = jnp.stack([pivots - col_start, row_pos - row_id * per_row, col_pos] + [pad] * 5)
    icol = jnp.stack([pivots - row_start, col_pos - col_id * wide, row_pos] + [pad] * 5, axis=1)

    in_panel = slot_ids % width
    coupled = pair_flags.astype(F32) * dinv_off
    zero = jnp.zeros_like(dinv_diag)
    coef = jnp.stack(
        [dinv_diag, jnp.where(in_panel == width - 1, 0.0, coupled), jnp.where(in_panel == 0, 0.0, jnp.roll(coupled, 1))]
        + [zero] * 5
    )
    row_in = jnp.any((row_start + jnp.arange(rows))[:, None] == pivots[None, :], axis=1)
    col_in = jnp.any((col_start + jnp.arange(cols))[:, None] == pivots[None, :], axis=1)
    row_keep = jnp.where(row_in, 0.0, 1.0)[:, None]
    col_keep = jnp.where(col_in, 0.0, 1.0)[None, :]

    dest_wide = jnp.broadcast_to(dest.astype(F32)[:, None], (nd, wide))
    raw, piv = pick_columns(front, delayed, dest_wide, irow, icol, wide, per_row)
    columns, side_hi, side_lo = gather(raw, piv, linv, coef, irow, icol, cols, per_row, nd)
    trailing, factor = update(columns, side_hi, side_lo, front, row_keep, col_keep)
    return (trailing, factor)


def solution(mesh):
    return jax.shard_map(
        body,
        mesh=mesh,
        in_specs=(P("row", "col"), P("col", "row"), P("col"), P(), P(), P(), P(), P()),
        out_specs=(P("row", "col"), P("row", None)),
        check_vma=False,
    )
```

```python
import functools

import jax
import jax.numpy as jnp
from jax import lax
from jax.experimental import pallas as pl
from jax.experimental.pallas import tpu as pltpu
from jax.sharding import PartitionSpec as P

MESH = pl.DeviceIdType.MESH
VMEM_LIMIT = 62 * 1024 * 1024
F32 = jnp.float32
BF16 = jnp.bfloat16
CHUNK = 256
COMM = 256
WIDE = 4
LANES = 128


def split(a):
    hi = a.astype(BF16)
    return hi, (a - hi.astype(F32)).astype(BF16)


def mm(a, b):
    return lax.dot_general(a, b, (((1,), (0,)), ((), ())), preferred_element_type=F32)


def mm_t(a, b):
    return lax.dot_general(a, b, (((1,), (1,)), ((), ())), preferred_element_type=F32)


def iota(shape, dim):
    return lax.broadcasted_iota(jnp.int32, shape, dim)


def one_hot(mask):
    return jnp.where(mask, 1.0, 0.0).astype(BF16)


def owner_of(ids, block, n):
    total = jnp.zeros(ids.shape, F32)
    for c in range(1, n):
        total += jnp.where(ids >= c * block, 1.0, 0.0)
    return total


def rank_of(owner_row, owner_col):
    slots = owner_row.shape[1]
    total = jnp.zeros((1, slots), F32)
    for t in range(slots // CHUNK):
        here = slice(t * CHUNK, (t + 1) * CHUNK)
        before = iota((CHUNK, slots), 0) + t * CHUNK < iota((CHUNK, slots), 1)
        same = owner_col[here, :] == owner_row
        total += jnp.sum(jnp.where(before & same, 1.0, 0.0), axis=0, keepdims=True)
    return total


def turned(row):
    return jnp.broadcast_to(row, (8, row.shape[1])).T[:, 0:1]


def pick_kernel(
    dims, front_ref, delayed_ref, dest_ref, ids_ref, dinv_ref,
    raw_ref, piv_ref, irow_ref, icol_ref, coef_ref, g_ref, want_ref, acc_ref, dacc_ref,
):
    n_row, n_col, rows, width, per_col = dims
    i = pl.program_id(0)
    slots = ids_ref.shape[1]
    cols, wide = g_ref.shape
    per_row = want_ref.shape[0]
    nd = delayed_ref.shape[0]
    tile = front_ref.shape[0]
    high = raw_ref.shape[1]
    ch = tile // raw_ref.shape[0]
    row_id, col_id = lax.axis_index("row"), lax.axis_index("col")

    @pl.when(i == 0)
    def _():
        piv = ids_ref[0:1, :].astype(F32)
        col_owner = owner_of(piv, cols, n_col)
        row_owner = owner_of(piv, rows, n_row)
        col_pos = col_owner * wide + rank_of(col_owner, turned(col_owner))
        row_pos = row_owner * per_row + rank_of(row_owner, turned(row_owner))
        piv_col = turned(piv)
        row_pos_col, col_pos_col = turned(row_pos), turned(col_pos)
        irow_ref[...] = jnp.zeros_like(irow_ref)
        irow_ref[0:1, :] = piv
        irow_ref[1:2, :] = col_pos
        icol_ref[...] = jnp.zeros_like(icol_ref)
        icol_ref[:, 0:1] = row_pos_col
        icol_ref[:, 1:2] = piv_col

        mine = col_pos_col - (col_id * wide).astype(F32) == iota((slots, wide), 1).astype(F32)
        want_col = jnp.sum(jnp.where(mine, piv_col - (col_id * cols).astype(F32), 0.0), axis=0, keepdims=True)
        real = iota((1, wide), 1) < per_col
        want_col = jnp.where(real, want_col, -1.0)
        g_ref[...] = one_hot(iota((cols, wide), 0).astype(F32) == want_col)
        mine = row_pos - (row_id * per_row).astype(F32) == iota((per_row, slots), 0).astype(F32)
        want_ref[...] = jnp.sum(jnp.where(mine, piv - (row_id * rows).astype(F32), 0.0), axis=1, keepdims=True)

        slot = iota((1, slots), 1) % width
        coupled = ids_ref[1:2, :].astype(F32) * dinv_ref[1:2, :]
        coef_ref[...] = jnp.zeros_like(coef_ref)
        coef_ref[0:1, :] = dinv_ref[0:1, :]
        coef_ref[1:2, :] = jnp.where(slot == width - 1, 0.0, coupled)
        coef_ref[2:3, :] = jnp.where(slot == 0, 0.0, pltpu.roll(jnp.broadcast_to(coupled, (8, slots)), 1, 1)[0:1, :])
        acc_ref[...] = jnp.zeros_like(acc_ref)
        dacc_ref[...] = jnp.zeros_like(dacc_ref)

    hi, lo = split(front_ref[...])
    g = g_ref[...]
    raw = mm(hi, g) + mm(lo, g)
    for b in range(raw_ref.shape[0]):
        raw_ref[b, :ch, :] = raw[b * ch : (b + 1) * ch, :]
        for t in range(ch // LANES):
            at = b * ch + t * LANES
            raw_ref[b, ch + t * nd : ch + (t + 1) * nd, :] = delayed_ref[:, at : at + LANES]

    start = row_tile(i, rows // tile, rows // cols) * tile
    sel = one_hot(want_ref[...].astype(jnp.int32) - start == iota((per_row, tile), 1))
    rh, rl = split(raw)
    acc_ref[...] += mm(sel, rh) + mm(sel, rl)
    dh, dl = split(delayed_ref[...])
    dacc_ref[...] += mm_t(dh, sel) + mm_t(dl, sel)

    @pl.when(i == pl.num_programs(0) - 1)
    def _():
        piv_ref[:per_row, :] = acc_ref[...]
        for b in range(per_row // LANES):
            piv_ref[per_row + b * nd : per_row + (b + 1) * nd, :] = dacc_ref[:, b * LANES : (b + 1) * LANES]
        diagonal = iota((nd, nd), 0) == iota((nd, nd), 1)
        dest = jnp.sum(jnp.where(diagonal, dest_ref[...].astype(F32), 0.0), axis=1, keepdims=True)
        piv_ref[per_row + per_row // LANES * nd :, :] = jnp.broadcast_to(dest, (nd, wide))


def row_tile(i, tiles, halves):
    return i % halves * (tiles // halves) + i // halves


def pick_columns(front, delayed, dest, ids, dinv, n_row, n_col, wide, width):
    rows, cols = front.shape
    nd = delayed.shape[0]
    slots = ids.shape[1]
    per_row = slots // n_row
    halves = rows // cols
    tile = CHUNK
    n = rows // tile
    sub = tile // COMM
    high = COMM + nd * (COMM // LANES)
    piv_high = per_row + nd * (per_row // LANES) + nd
    dims = (n_row, n_col, rows, width, slots // n_col)
    return pl.pallas_call(
        functools.partial(pick_kernel, dims),
        grid=(n,),
        in_specs=[
            pl.BlockSpec((tile, cols), lambda i: (row_tile(i, n, halves), 0)),
            pl.BlockSpec((nd, tile), lambda i: (0, row_tile(i, n, halves))),
            pl.BlockSpec((1, nd), lambda i: (0, 0)),
            pl.BlockSpec((2, slots), lambda i: (0, 0)),
            pl.BlockSpec((2, slots), lambda i: (0, 0)),
        ],
        out_specs=(
            pl.BlockSpec((sub, high, wide), lambda i: (i, 0, 0)),
            pl.BlockSpec((piv_high, wide), lambda i: (0, 0)),
            pl.BlockSpec((8, slots), lambda i: (0, 0)),
            pl.BlockSpec((slots, 8), lambda i: (0, 0)),
            pl.BlockSpec((8, slots), lambda i: (0, 0)),
        ),
        out_shape=(
            jax.ShapeDtypeStruct((n * sub, high, wide), F32),
            jax.ShapeDtypeStruct((piv_high, wide), F32),
            jax.ShapeDtypeStruct((8, slots), F32),
            jax.ShapeDtypeStruct((slots, 8), F32),
            jax.ShapeDtypeStruct((8, slots), F32),
        ),
        scratch_shapes=[
            pltpu.VMEM((cols, wide), BF16),
            pltpu.VMEM((per_row, 1), F32),
            pltpu.VMEM((per_row, wide), F32),
            pltpu.VMEM((nd, per_row), F32),
        ],
        compiler_params=pltpu.CompilerParams(dimension_semantics=("arbitrary",), vmem_limit_bytes=VMEM_LIMIT),
    )(front, delayed, dest, ids, dinv)


def gather_kernel(
    dims, raw_own, piv_own, linv_ref, coef_ref, irow_ref, icol_ref,
    cols_out, hi_out, lo_out, rkeep_ref, ckeep_ref,
    raw_all, col_raw, piv_all, rowperm, t1h, t1l, qh, ql, nh, nl, rd, mh, ml, stage, stage_h, stage_l,
    keep_sem, root_sem, raw_recv, raw_send, col_recv, col_send, piv_recv, piv_send, out_sem, hi_sem, lo_sem,
):
    zs, xs, ys, halves, per_row, nd, x_rows = dims
    nc, n_row = zs * xs, ys * 2
    nch = raw_own.shape[0]
    high = raw_own.shape[1]
    hch = nch // halves
    panels, width, _ = linv_ref.shape
    slots = panels * width
    wide = raw_own.shape[2]
    ch = COMM
    sub = CHUNK // COMM
    z_part, x_part = pl.ds(0, high - x_rows), pl.ds(high - x_rows, x_rows)
    kraw = nc * wide
    row, col = lax.axis_index("row"), lax.axis_index("col")
    y, k = row // 2, row % 2
    z, x = col // xs, col % xs
    root = col // halves
    half = col % halves
    root_y, root_k = root // 2, root % 2
    is_root = row == root
    at_root_core = k == root_k
    reach = zs + xs - 2
    span = reach + ys - 1

    def at(y_, k_, z_, x_):
        return (y_ * 2 + k_, z_ * xs + x_)

    links = [
        (z + 1 < zs, at(y, k, z + 1, x)),
        (z >= 1, at(y, k, z - 1, x)),
        (x + 1 < xs, at(y, k, z, x + 1)),
        (x >= 1, at(y, k, z, x - 1)),
        (y + 1 < ys, at(y + 1, k, z, x)),
        (y >= 1, at(y - 1, k, z, x)),
        (None, at(y, 1 - k, z, x)),
    ]

    barrier = pltpu.get_barrier_semaphore()
    peers = 1
    for cond, dev in links:
        if cond is None:
            pl.semaphore_signal(barrier, inc=1, device_id=dev, device_id_type=MESH)
        else:
            peers = peers + jnp.where(cond, 1, 0)

            @pl.when(cond)
            def _(dev=dev):
                pl.semaphore_signal(barrier, inc=1, device_id=dev, device_id_type=MESH)
    pl.semaphore_wait(barrier, peers)

    def remote(way, src, dst, send, recv):
        return pltpu.make_async_remote_copy(
            src_ref=src, dst_ref=dst, send_sem=send, recv_sem=recv, device_id=links[way][1], device_id_type=MESH)

    def piv_ways(sy, c):
        zc, xc = c // xs, c % xs
        same_y = sy == y
        same_x = xc == x
        return [
            (0, (z + 1 < zs) & (zc <= z) & same_x & same_y),
            (1, (z >= 1) & (zc >= z) & same_x & same_y),
            (2, (x + 1 < xs) & (xc <= x) & same_y),
            (3, (x >= 1) & (xc >= x) & same_y),
            (4, (y + 1 < ys) & (sy <= y)),
            (5, (y >= 1) & (sy >= y)),
        ]

    def piv_copy(way, sy, c, src):
        s = sy * 2 + k
        return remote(way, src, piv_all.at[s, c], piv_send.at[way, sy * nc + c], piv_recv.at[s, c])

    def piv_arrived(s, c):
        pltpu.make_async_copy(piv_all.at[s, c], piv_all.at[s, c], piv_recv.at[s, c]).wait()

    def piv_step(sy, c, src):
        for way, cond in piv_ways(sy, c):
            @pl.when(cond)
            def _(way=way):
                piv_copy(way, sy, c, src).start()
        piv_copy(6, sy, c, src).start()

    def raw_ways(c):
        zc, xc = c // xs, c % xs
        same_x, same_z = xc == x, zc == z
        return [
            (0, (z + 1 < zs) & (zc <= z), same_x, x_part),
            (1, (z >= 1) & (zc >= z), same_x, x_part),
            (2, (x + 1 < xs) & (xc <= x), same_z, z_part),
            (3, (x >= 1) & (xc >= x), same_z, z_part),
        ]

    def side_of(i):
        e = i // sub
        return e // halves * sub + i % sub, (i >= 0) & (i < nch) & (e % halves == half)

    def raw_arrived(c, i):
        line = (c // xs == z) | (c % xs == x)
        whole = raw_all.at[c, i]

        @pl.when(line)
        def _():
            pltpu.make_async_copy(whole, whole, raw_recv.at[c, i, 0]).wait()

        @pl.when(jnp.logical_not(line))
        def _():
            for n, part in enumerate((z_part, x_part)):
                ref = raw_all.at[c, i, part]
                pltpu.make_async_copy(ref, ref, raw_recv.at[c, i, n]).wait()

    def col_copy(way, c, j, src):
        return remote(way, src, col_raw.at[c, j], col_send.at[way - 4, c], col_recv.at[c, j])

    def raw_step(c, i, src):
        for way, cond, line, part in raw_ways(c):
            @pl.when(cond & line)
            def _(way=way):
                remote(way, src, raw_all.at[c, i], raw_send.at[way, c], raw_recv.at[c, i, 0]).start()

            @pl.when(cond & jnp.logical_not(line))
            def _(way=way, part=part):
                remote(
                    way, src.at[part], raw_all.at[c, i, part],
                    raw_send.at[way, c], raw_recv.at[c, i, 1 if way < 2 else 0]).start()
        j, mine = side_of(i)

        @pl.when(is_root & mine)
        def _():
            @pl.when(y + 1 < ys)
            def _():
                col_copy(4, c, j, src).start()

            @pl.when(y >= 1)
            def _():
                col_copy(5, c, j, src).start()
            col_copy(6, c, j, src).start()
            pltpu.make_async_copy(src, col_raw.at[c, j], root_sem.at[c, j]).start()

    def col_arrived(c, j):
        pltpu.make_async_copy(col_raw.at[c, j], col_raw.at[c, j], col_recv.at[c, j]).wait()

    keep_raw = pltpu.make_async_copy(raw_own, raw_all.at[col], keep_sem.at[0])
    keep_piv = pltpu.make_async_copy(piv_own, piv_all.at[row, col], keep_sem.at[1])
    keep_raw.start()
    keep_piv.start()

    def own_step(i):
        @pl.when(i < nch)
        def _():
            raw_step(col, i, raw_own.at[i])

    piv_step(y, col, piv_own)
    own_step(0)
    ahead = 1

    @pl.loop(1, span + 1)
    def _(s):
        @pl.loop(0, ys * nc)
        def _(q):
            sy, c = q // nc, q % nc
            dist = jnp.abs(c // xs - z) + jnp.abs(c % xs - x) + jnp.abs(sy - y)

            @pl.when(dist == s)
            def _():
                piv_arrived(sy * 2 + k, c)
                piv_step(sy, c, piv_all.at[sy * 2 + k, c])
        own_step(s)
    ahead = span + 1

    def panel(p, n=1):
        return slice(p * width, (p + n) * width)

    def masks():
        n = ckeep_ref.shape[1] // CHUNK

        @pl.loop(0, n)
        def _(t):
            ids = iota((slots, CHUNK), 1) + t * CHUNK + col * (n * CHUNK)
            hit = jnp.where(icol_ref[:, 1:2].astype(jnp.int32) == ids, 1.0, 0.0)
            ckeep_ref[:, pl.ds(pl.multiple_of(t * CHUNK, CHUNK), CHUNK)] = 1.0 - jnp.max(hit, axis=0, keepdims=True)
        n = rkeep_ref.shape[0] // CHUNK

        @pl.loop(0, n)
        def _(t):
            ids = iota((CHUNK, slots), 0) + t * CHUNK + row * (n * CHUNK)
            hit = jnp.where(irow_ref[0:1, :].astype(jnp.int32) == ids, 1.0, 0.0)
            rkeep_ref[pl.ds(pl.multiple_of(t * CHUNK, CHUNK), CHUNK), :] = 1.0 - jnp.max(hit, axis=1, keepdims=True)

    def gather_square():
        @pl.loop(0, ys * nc)
        def _(q):
            piv_arrived((q // nc) * 2 + 1 - k, q % nc)
        keep_piv.wait()

        @pl.loop(0, panels - 1)
        def _(p):
            part = pl.ds(pl.multiple_of(p * width, width), width)
            later = pl.ds(pl.multiple_of((p + 1) * width, width), width)
            rowperm[part, :] = one_hot(icol_ref[later, 0:1].astype(jnp.int32) == iota((width, n_row * per_row), 1))

        @pl.loop(0, nc // 2)
        def _(c2):
            block = jnp.concatenate(
                [
                    jnp.concatenate([piv_all[r, c2 * 2 + b, :per_row, :] for b in range(2)], axis=1)
                    for r in range(n_row)
                ],
                axis=0,
            )
            h, l = split(block)
            at_cols = pl.ds(pl.multiple_of(c2 * 2 * wide, 2 * wide), 2 * wide)

            @pl.loop(0, panels - 1)
            def _(p):
                part = pl.ds(pl.multiple_of(p * width, width), width)
                perm = rowperm[part, :]
                a, b = split(mm(perm, h) + mm(perm, l))
                t1h[part, at_cols] = a
                t1l[part, at_cols] = b
        rest = [
            jnp.concatenate(
                [
                    piv_all[r, c, per_row + b * nd : per_row + (b + 1) * nd, :]
                    for r in range(n_row)
                    for b in range(per_row // LANES)
                ],
                axis=1,
            )
            for c in range(nc)
        ]
        h, l = split(jnp.concatenate(rest, axis=0))

        @pl.loop(0, panels - 1)
        def _(p):
            part = pl.ds(pl.multiple_of(p * width, width), width)
            perm = rowperm[part, :]
            a, b = split(mm_t(perm, h) + mm_t(perm, l))
            t1h[part, kraw:] = a
            t1l[part, kraw:] = b

    def dests():
        return jnp.concatenate(
            [piv_all[0, c, per_row + per_row // LANES * nd :, 0:1] for c in range(nc)], axis=0
        ).astype(jnp.int32)

    def square():
        d = dests()

        @pl.loop(0, panels - 1)
        def _(p):
            part = pl.ds(pl.multiple_of(p * width, width), width)
            slot = irow_ref[1:2, part].astype(jnp.int32)
            take = one_hot(slot == iota((kraw, width), 0))
            put = one_hot(d == iota((nc * nd, width), 1) + p * width)
            take = jnp.concatenate([take, put], axis=0)

            @pl.loop(0, panels - 1)
            def _(r):
                rows = pl.ds(pl.multiple_of(r * width, width), width)
                h, l = split(mm(t1h[rows, :], take) + mm(t1l[rows, :], take))
                qh[rows, part] = h
                ql[rows, part] = l

    def dot3(a, b, f):
        return f(a[0], b[0]) + f(a[0], b[1]) + f(a[1], b[0])

    def recur():
        nh[...] = jnp.zeros_like(nh)
        nl[...] = jnp.zeros_like(nl)
        for p in range(panels):
            mine = split(linv_ref[p])
            nh[panel(p), panel(p)], nl[panel(p), panel(p)] = mine
            if p == 0:
                continue
            e, until = p - 1, slice(0, p * width)
            for q in range(p, panels):
                rows = panel(q - 1)
                r = dot3((qh[rows, until], ql[rows, until]), (nh[panel(e), until], nl[panel(e), until]), mm_t)
                rd[rows, panel(e)] = pair_scale(r, coef_ref, panel(e))
            b = dot3(mine, split(rd[panel(p - 1), until]), mm)
            out = dot3(split(-b), (nh[until, until], nl[until, until]), mm)
            nh[panel(p), until], nl[panel(p), until] = split(out)

    def spread():
        step = 2 * wide

        @pl.loop(0, kraw // step)
        def _(t):
            part = pl.ds(pl.multiple_of(t * step, step), step)
            take = one_hot(irow_ref[1:2, :].astype(jnp.int32) == iota((step, slots), 0) + t * step)
            mh[part, :] = mm_t(take, nh[...]).astype(BF16)
            ml[part, :] = mm_t(take, nl[...]).astype(BF16)
        put = one_hot(dests() == iota((nc * nd, slots), 1))
        h = mm_t(put, nh[...]).astype(BF16)
        mh[kraw:, :] = jnp.concatenate([h, mm_t(put, nl[...]).astype(BF16), h], axis=0)

    def chunk_parts(ref, e):
        blocks = [e * sub + b for b in range(sub)]
        a = jnp.concatenate(
            [jnp.concatenate([ref[c, i, :ch, :] for c in range(nc)], axis=1) for i in blocks], axis=0)
        d = jnp.concatenate(
            [
                jnp.concatenate(
                    [ref[c, i, ch + b * nd : ch + (b + 1) * nd, :] for i in blocks for b in range(ch // LANES)], axis=1)
                for c in range(nc)
            ],
            axis=0,
        )
        dh, dl = split(d.T)
        ah, al = split(a)
        return jnp.concatenate([ah, dh, dh, dl], axis=1), ah, al

    def scaled_tile(parts, part):
        return mm(parts[0], mh[:, part]) + mm(parts[1], ml[:, part]) + mm(parts[2], mh[:kraw, part])

    def cols_copy(e):
        rows = pl.ds(pl.multiple_of(row_tile(e, nch // sub, halves) * CHUNK, CHUNK), CHUNK)
        return pltpu.make_async_copy(stage.at[e % 2], cols_out.at[rows, :], out_sem.at[e % 2])

    def eliminate(e):
        @pl.when(e >= 2)
        def _():
            cols_copy(e - 2).wait()
        parts = chunk_parts(raw_all, e)
        for p in range(0, panels, WIDE):
            scaled = scaled_tile(parts, panel(p, WIDE))
            stage[e % 2, :, panel(p, WIDE)] = pair_scale(scaled, coef_ref, panel(p, WIDE))
        cols_copy(e).start()

    def side_copies(e):
        cols = pl.ds(pl.multiple_of(e * CHUNK, CHUNK), CHUNK)
        return (
            pltpu.make_async_copy(stage_h.at[e % 2], hi_out.at[:, cols], hi_sem.at[e % 2]),
            pltpu.make_async_copy(stage_l.at[e % 2], lo_out.at[:, cols], lo_sem.at[e % 2]),
        )

    def eliminate_side(e):
        @pl.when(k != root_k)
        def _():
            @pl.loop(0, nc)
            def _(c):
                for b in range(sub):
                    col_arrived(c, e * sub + b)

        @pl.when(is_root)
        def _():
            @pl.loop(0, nc)
            def _(c):
                for b in range(sub):
                    ref = col_raw.at[c, e * sub + b]
                    pltpu.make_async_copy(ref, ref, root_sem.at[c, e * sub + b]).wait()

        @pl.when(e >= 2)
        def _():
            for copy in side_copies(e - 2):
                copy.wait()
        parts = chunk_parts(col_raw, e)
        for p in range(0, panels, WIDE):
            stage_h[e % 2, panel(p, WIDE), :], stage_l[e % 2, panel(p, WIDE), :] = split(
                scaled_tile(parts, panel(p, WIDE)).T)
        for copy in side_copies(e):
            copy.start()

    first = max(reach - 1, 3)
    side_lag = reach - 1 + ys
    work = [gather_square, square, recur]

    @pl.loop(0, nch + max(first, side_lag))
    def _(s):
        own_step(s + ahead)

        @pl.loop(0, nc)
        def _(c):
            dist = jnp.abs(c // xs - z) + jnp.abs(c % xs - x)
            i = s - (dist - 1)

            @pl.when((dist >= 1) & (i >= 0) & (i < nch))
            def _():
                raw_arrived(c, i)
                raw_step(c, i, raw_all.at[c, i])

        @pl.when(at_root_core & (y != root_y))
        def _():
            @pl.loop(0, nc)
            def _(c):
                dist = jnp.abs(c // xs - z) + jnp.abs(c % xs - x)
                j, mine = side_of(s - (jnp.maximum(dist, 1) - 1) - jnp.abs(y - root_y))

                @pl.when(mine)
                def _():
                    col_arrived(c, j)
                    src = col_raw.at[c, j]

                    @pl.when((y > root_y) & (y + 1 < ys))
                    def _():
                        col_copy(4, c, j, src).start()

                    @pl.when((y < root_y) & (y >= 1))
                    def _():
                        col_copy(5, c, j, src).start()
                    col_copy(6, c, j, src).start()

        for n, piece in enumerate(work):
            pl.when(s == n)(piece)

        @pl.when(s == len(work) - 1)
        def _():
            spread()
            masks()
            keep_raw.wait()

        i = s - first

        @pl.when((i >= 0) & (i < nch) & (i % sub == sub - 1))
        def _():
            eliminate(i // sub)
        j, mine = side_of(s - side_lag)

        @pl.when(mine & (j % sub == sub - 1))
        def _():
            eliminate_side(j // sub)

    for e in range(max(nch // sub - 2, 0), nch // sub):
        cols_copy(e).wait()
    for e in range(max(hch // sub - 2, 0), hch // sub):
        for copy in side_copies(e):
            copy.wait()

    @pl.loop(0, ys * nc)
    def _(q):
        sy, c = q // nc, q % nc
        for way, cond in piv_ways(sy, c):
            @pl.when(cond)
            def _(way=way):
                piv_copy(way, sy, c, piv_own).wait_send()
        piv_copy(6, sy, c, piv_own).wait_send()

    def sent(ref, sem):
        pltpu.make_async_copy(ref, ref, sem).wait()

    @pl.loop(0, nc)
    def _(c):
        for way, cond, line, part in raw_ways(c):
            @pl.when(cond & line)
            def _(way=way):
                sent(raw_all.at[c], raw_send.at[way, c])

            @pl.when(cond & jnp.logical_not(line))
            def _(way=way, part=part):
                sent(raw_all.at[c, :, part], raw_send.at[way, c])

        @pl.when(is_root | (at_root_core & (y > root_y)))
        def _():
            @pl.when(y + 1 < ys)
            def _():
                sent(col_raw.at[c], col_send.at[0, c])

        @pl.when(is_root | (at_root_core & (y < root_y)))
        def _():
            @pl.when(y >= 1)
            def _():
                sent(col_raw.at[c], col_send.at[1, c])

        @pl.when(at_root_core)
        def _():
            sent(col_raw.at[c], col_send.at[2, c])


def pair_scale(scaled, coef_ref, part):
    width = scaled.shape[1]
    return (
        scaled * coef_ref[0:1, part]
        + pltpu.roll(scaled, width - 1, 1) * coef_ref[1:2, part]
        + pltpu.roll(scaled, 1, 1) * coef_ref[2:3, part]
    )


def gather(raw, piv, linv, coef, irow, icol, cols, per_row, nd):
    n_col = lax.axis_size("col")
    n_row = lax.axis_size("row")
    nch, high, wide = raw.shape
    panels, width, _ = linv.shape
    slots = panels * width
    rows = nch * COMM
    halves = rows // cols
    ys = n_row // 2
    xs = ys if n_col % ys == 0 else 1
    zs = n_col // xs
    hch = nch // halves
    x_rows = (high + 47) // 48 * 8
    kraw = n_col * wide
    kall = kraw + n_col * nd
    early = slots - width
    vmem = pl.BlockSpec(memory_space=pltpu.VMEM)
    hbm = pl.BlockSpec(memory_space=pl.ANY)
    dma = pltpu.SemaphoreType.DMA
    return pl.pallas_call(
        functools.partial(gather_kernel, (zs, xs, ys, halves, per_row, nd, x_rows)),
        out_shape=(
            jax.ShapeDtypeStruct((rows, slots), F32),
            jax.ShapeDtypeStruct((slots, cols), BF16),
            jax.ShapeDtypeStruct((slots, cols), BF16),
            jax.ShapeDtypeStruct((rows, 1), F32),
            jax.ShapeDtypeStruct((1, cols), F32),
        ),
        in_specs=[vmem] * 6,
        out_specs=(hbm, hbm, hbm, vmem, vmem),
        scratch_shapes=[
            pltpu.VMEM((n_col, nch, high, wide), F32),
            pltpu.VMEM((n_col, hch, high, wide), F32),
            pltpu.VMEM((n_row, n_col) + piv.shape, F32),
            pltpu.VMEM((early, slots), BF16),
            pltpu.VMEM((early, kall), BF16),
            pltpu.VMEM((early, kall), BF16),
            pltpu.VMEM((early, early), BF16),
            pltpu.VMEM((early, early), BF16),
            pltpu.VMEM((slots, slots), BF16),
            pltpu.VMEM((slots, slots), BF16),
            pltpu.VMEM((early, early), F32),
            pltpu.VMEM((kraw + 3 * n_col * nd, slots), BF16),
            pltpu.VMEM((kraw, slots), BF16),
            pltpu.VMEM((2, CHUNK, slots), F32),
            pltpu.VMEM((2, slots, CHUNK), BF16),
            pltpu.VMEM((2, slots, CHUNK), BF16),
            dma((2,)),
            dma((n_col, hch)),
            dma((n_col, nch, 2)),
            dma((4, n_col)),
            dma((n_col, hch)),
            dma((3, n_col)),
            dma((n_row, n_col)),
            dma((7, ys * n_col)),
            dma((2,)),
            dma((2,)),
            dma((2,)),
        ],
        compiler_params=pltpu.CompilerParams(
            collective_id=0, has_side_effects=True, vmem_limit_bytes=VMEM_LIMIT
        ),
    )(raw, piv, linv, coef, irow, icol)


def trailing_kernel(c_ref, hi_ref, lo_ref, front_ref, rkeep_ref, ckeep_ref, out_ref, factor_ref):
    columns = c_ref[...]
    factor_ref[...] = columns
    hi, lo = split(columns)
    bh = hi_ref[...]
    acc = mm(hi, bh) + mm(hi, lo_ref[...]) + mm(lo, bh)
    keep = (rkeep_ref[...] > 0.0) & (ckeep_ref[...] > 0.0)
    out_ref[...] = jnp.where(keep, front_ref[...] - acc, 0.0)


def update(columns, side_hi, side_lo, front, row_keep, col_keep):
    rows, cols = front.shape
    slots = columns.shape[1]
    tile = 256
    return pl.pallas_call(
        trailing_kernel,
        grid=(rows // tile,),
        in_specs=[
            pl.BlockSpec((tile, slots), lambda i: (i, 0)),
            pl.BlockSpec((slots, cols), lambda i: (0, 0)),
            pl.BlockSpec((slots, cols), lambda i: (0, 0)),
            pl.BlockSpec((tile, cols), lambda i: (i, 0)),
            pl.BlockSpec((tile, 1), lambda i: (i, 0)),
            pl.BlockSpec((1, cols), lambda i: (0, 0)),
        ],
        out_specs=(
            pl.BlockSpec((tile, cols), lambda i: (i, 0)),
            pl.BlockSpec((tile, slots), lambda i: (i, 0)),
        ),
        out_shape=(
            jax.ShapeDtypeStruct((rows, cols), F32),
            jax.ShapeDtypeStruct((rows, slots), F32),
        ),
        compiler_params=pltpu.CompilerParams(dimension_semantics=("arbitrary",), vmem_limit_bytes=VMEM_LIMIT),
    )(columns, side_hi, side_lo, front, row_keep, col_keep)


def body(front, delayed, dest, pivots, pair_flags, linv, dinv_diag, dinv_off):
    n_col = lax.axis_size("col")
    n_row = lax.axis_size("row")
    rows, cols = front.shape
    panels, width, _ = linv.shape
    slots = pivots.shape[0]
    per_col = slots // n_col
    per_row = slots // n_row
    wide = (per_col + LANES - 1) // LANES * LANES
    nd = delayed.shape[0]
    ids = jnp.stack([pivots, pair_flags])
    dinv = jnp.stack([dinv_diag, dinv_off])
    raw, piv, irow, icol, coef = pick_columns(front, delayed, dest[None, :], ids, dinv, n_row, n_col, wide, width)
    columns, side_hi, side_lo, row_keep, col_keep = gather(raw, piv, linv, coef, irow, icol, cols, per_row, nd)
    trailing, factor = update(columns, side_hi, side_lo, front, row_keep, col_keep)
    return (trailing, factor)


def solution(mesh):
    return jax.shard_map(
        body,
        mesh=mesh,
        in_specs=(P("row", "col"), P("col", "row"), P("col"), P(), P(), P(), P(), P()),
        out_specs=(P("row", "col"), P("row", None)),
        check_vma=False,
    )
```

```python
import functools

import jax
import jax.numpy as jnp
from jax import lax
from jax.experimental import pallas as pl
from jax.experimental.pallas import tpu as pltpu
from jax.sharding import PartitionSpec as P

MESH = pl.DeviceIdType.MESH
VMEM_LIMIT = 66_800_000
F32 = jnp.float32
BF16 = jnp.bfloat16
CHUNK = 256
COMM = 256
EARLY = 4
WIDE = 4
LANES = 128


def split(a):
    hi = a.astype(BF16)
    return hi, (a - hi.astype(F32)).astype(BF16)


def mm(a, b):
    return lax.dot_general(a, b, (((1,), (0,)), ((), ())), preferred_element_type=F32)


def mm_t(a, b):
    return lax.dot_general(a, b, (((1,), (1,)), ((), ())), preferred_element_type=F32)


def iota(shape, dim):
    return lax.broadcasted_iota(jnp.int32, shape, dim)


def one_hot(mask):
    return jnp.where(mask, 1.0, 0.0).astype(BF16)


def owner_of(ids, block, n):
    total = jnp.zeros(ids.shape, F32)
    for c in range(1, n):
        total += jnp.where(ids >= c * block, 1.0, 0.0)
    return total


def rank_of(owner_row, owner_col):
    slots = owner_row.shape[1]
    total = jnp.zeros((1, slots), F32)
    for t in range(slots // CHUNK):
        here = slice(t * CHUNK, (t + 1) * CHUNK)
        before = iota((CHUNK, slots), 0) + t * CHUNK < iota((CHUNK, slots), 1)
        same = owner_col[here, :] == owner_row
        total += jnp.sum(jnp.where(before & same, 1.0, 0.0), axis=0, keepdims=True)
    return total


def turned(row):
    return jnp.broadcast_to(row, (8, row.shape[1])).T[:, 0:1]


def index_tables(dims, row_id, col_id, ids_ref, dinv_ref, irow_ref, icol_ref, coef_ref, g_ref, want_ref):
    n_row, n_col, rows, cols, width, per_col = dims
    slots = ids_ref.shape[1]
    wide = g_ref.shape[1]
    per_row = want_ref.shape[0]
    piv = ids_ref[0:1, :].astype(F32)
    col_owner = owner_of(piv, cols, n_col)
    row_owner = owner_of(piv, rows, n_row)
    col_pos = col_owner * wide + rank_of(col_owner, turned(col_owner))
    row_pos = row_owner * per_row + rank_of(row_owner, turned(row_owner))
    piv_col = turned(piv)
    col_pos_col = turned(col_pos)
    irow_ref[...] = jnp.zeros_like(irow_ref)
    irow_ref[0:1, :] = piv
    irow_ref[1:2, :] = col_pos
    icol_ref[...] = jnp.zeros_like(icol_ref)
    icol_ref[:, 0:1] = turned(row_pos)
    icol_ref[:, 1:2] = piv_col

    mine = col_pos_col - (col_id * wide).astype(F32) == iota((slots, wide), 1).astype(F32)
    want_col = jnp.sum(jnp.where(mine, piv_col - (col_id * cols).astype(F32), 0.0), axis=0, keepdims=True)
    want_col = jnp.where(iota((1, wide), 1) < per_col, want_col, -1.0)
    g_ref[...] = one_hot(iota((cols, wide), 0).astype(F32) == want_col)
    mine = row_pos - (row_id * per_row).astype(F32) == iota((per_row, slots), 0).astype(F32)
    want_ref[...] = jnp.sum(jnp.where(mine, piv - (row_id * rows).astype(F32), 0.0), axis=1, keepdims=True)

    slot = iota((1, slots), 1) % width
    coupled = ids_ref[1:2, :].astype(F32) * dinv_ref[1:2, :]
    coef_ref[...] = jnp.zeros_like(coef_ref)
    coef_ref[0:1, :] = dinv_ref[0:1, :]
    coef_ref[1:2, :] = jnp.where(slot == width - 1, 0.0, coupled)
    coef_ref[2:3, :] = jnp.where(slot == 0, 0.0, pltpu.roll(jnp.broadcast_to(coupled, (8, slots)), 1, 1)[0:1, :])


def row_tile(i, tiles, halves):
    return i % halves * (tiles // halves) + i // halves


def gather_kernel(
    dims, front_ref, delayed_ref, dest_ref, ids_ref, dinv_ref, linv_ref,
    cols_out, hi_out, lo_out, rkeep_ref, ckeep_ref,
    irow_ref, icol_ref, coef_ref, g_ref, want_ref, acc_ref, dacc_ref, fbuf,
    raw_all, col_raw, piv_all, rowperm, t1h, t1l, qh, ql, nh, nl, rd, mh, ml, stage, stage_h, stage_l,
    front_sem, root_sem, raw_recv, raw_send, col_recv, col_send, piv_recv, piv_send, out_sem, hi_sem, lo_sem,
):
    zs, xs, ys, halves, per_row, nd, x_rows = dims
    nc, n_row = zs * xs, ys * 2
    nch, high, wide = raw_all.shape[1:]
    rows, cols = front_ref.shape
    hch = nch // halves
    panels, width, _ = linv_ref.shape
    slots = panels * width
    ch = COMM
    sub = CHUNK // COMM
    z_part, x_part = pl.ds(0, high - x_rows), pl.ds(high - x_rows, x_rows)
    kraw = nc * wide
    row, col = lax.axis_index("row"), lax.axis_index("col")
    y, k = row // 2, row % 2
    z, x = col // xs, col % xs
    root = col // halves
    half = col % halves
    root_y, root_k = root // 2, root % 2
    is_root = row == root
    at_root_core = k == root_k
    reach = zs + xs - 2
    span = reach + ys - 1

    def at(y_, k_, z_, x_):
        return (y_ * 2 + k_, z_ * xs + x_)

    links = [
        (z + 1 < zs, at(y, k, z + 1, x)),
        (z >= 1, at(y, k, z - 1, x)),
        (x + 1 < xs, at(y, k, z, x + 1)),
        (x >= 1, at(y, k, z, x - 1)),
        (y + 1 < ys, at(y + 1, k, z, x)),
        (y >= 1, at(y - 1, k, z, x)),
        (None, at(y, 1 - k, z, x)),
    ]

    for i in range(min(2, nch)):
        tile = pl.ds(row_tile(i, nch, halves) * CHUNK, CHUNK)
        pltpu.make_async_copy(front_ref.at[tile, :], fbuf.at[i], front_sem.at[i]).start()

    barrier = pltpu.get_barrier_semaphore()
    peers = 1
    for cond, dev in links:
        if cond is None:
            pl.semaphore_signal(barrier, inc=1, device_id=dev, device_id_type=MESH)
        else:
            peers = peers + jnp.where(cond, 1, 0)

            @pl.when(cond)
            def _(dev=dev):
                pl.semaphore_signal(barrier, inc=1, device_id=dev, device_id_type=MESH)
    pl.semaphore_wait(barrier, peers)

    def remote(way, src, dst, send, recv):
        return pltpu.make_async_remote_copy(
            src_ref=src, dst_ref=dst, send_sem=send, recv_sem=recv, device_id=links[way][1], device_id_type=MESH)

    def piv_ways(sy, c):
        zc, xc = c // xs, c % xs
        same_y = sy == y
        same_x = xc == x
        return [
            (0, (z + 1 < zs) & (zc <= z) & same_x & same_y),
            (1, (z >= 1) & (zc >= z) & same_x & same_y),
            (2, (x + 1 < xs) & (xc <= x) & same_y),
            (3, (x >= 1) & (xc >= x) & same_y),
            (4, (y + 1 < ys) & (sy <= y)),
            (5, (y >= 1) & (sy >= y)),
        ]

    def piv_copy(way, sy, c, src):
        s = sy * 2 + k
        return remote(way, src, piv_all.at[s, c], piv_send.at[way, sy * nc + c], piv_recv.at[s, c])

    def piv_arrived(s, c):
        pltpu.make_async_copy(piv_all.at[s, c], piv_all.at[s, c], piv_recv.at[s, c]).wait()

    def piv_step(sy, c, src):
        for way, cond in piv_ways(sy, c):
            @pl.when(cond)
            def _(way=way):
                piv_copy(way, sy, c, src).start()
        piv_copy(6, sy, c, src).start()

    def raw_ways(c):
        zc, xc = c // xs, c % xs
        same_x, same_z = xc == x, zc == z
        return [
            (0, (z + 1 < zs) & (zc <= z), same_x, x_part),
            (1, (z >= 1) & (zc >= z), same_x, x_part),
            (2, (x + 1 < xs) & (xc <= x), same_z, z_part),
            (3, (x >= 1) & (xc >= x), same_z, z_part),
        ]

    def side_of(i):
        e = i // sub
        return e // halves * sub + i % sub, (i >= 0) & (i < nch) & (e % halves == half)

    def raw_arrived(c, i):
        line = (c // xs == z) | (c % xs == x)
        whole = raw_all.at[c, i]

        @pl.when(line)
        def _():
            pltpu.make_async_copy(whole, whole, raw_recv.at[c, i, 0]).wait()

        @pl.when(jnp.logical_not(line))
        def _():
            for n, part in enumerate((z_part, x_part)):
                ref = raw_all.at[c, i, part]
                pltpu.make_async_copy(ref, ref, raw_recv.at[c, i, n]).wait()

    def col_copy(way, c, j, src):
        return remote(way, src, col_raw.at[c, j], col_send.at[way - 4, c], col_recv.at[c, j])

    def raw_step(c, i, src):
        for way, cond, line, part in raw_ways(c):
            @pl.when(cond & line)
            def _(way=way):
                remote(way, src, raw_all.at[c, i], raw_send.at[way, c], raw_recv.at[c, i, 0]).start()

            @pl.when(cond & jnp.logical_not(line))
            def _(way=way, part=part):
                remote(
                    way, src.at[part], raw_all.at[c, i, part],
                    raw_send.at[way, c], raw_recv.at[c, i, 1 if way < 2 else 0]).start()
        j, mine = side_of(i)

        @pl.when(is_root & mine)
        def _():
            @pl.when(y + 1 < ys)
            def _():
                col_copy(4, c, j, src).start()

            @pl.when(y >= 1)
            def _():
                col_copy(5, c, j, src).start()
            col_copy(6, c, j, src).start()
            pltpu.make_async_copy(src, col_raw.at[c, j], root_sem.at[c, j]).start()

    def col_arrived(c, j):
        pltpu.make_async_copy(col_raw.at[c, j], col_raw.at[c, j], col_recv.at[c, j]).wait()

    own_piv = piv_all.at[row, col]

    def own_step(i):
        @pl.when(i < nch)
        def _():
            raw_step(col, i, raw_all.at[col, i])

    def front_copy(i):
        tile = pl.ds(pl.multiple_of(row_tile(i, nch, halves) * CHUNK, CHUNK), CHUNK)
        return pltpu.make_async_copy(front_ref.at[tile, :], fbuf.at[i % 3], front_sem.at[i % 3])

    def pick(i):
        hi, lo = split(fbuf[i % 3])
        g = g_ref[...]
        raw_all[col, i, :ch, :] = mm(hi, g) + mm(lo, g)
        start = row_tile(i, nch, halves) * CHUNK
        for t in range(ch // LANES):
            part = pl.ds(pl.multiple_of(start + t * LANES, LANES), LANES)
            raw_all[col, i, ch + t * nd : ch + (t + 1) * nd, :] = delayed_ref[:, part]

    def pick_rows(i):
        start = row_tile(i, nch, halves) * CHUNK
        sel = one_hot(want_ref[...].astype(jnp.int32) - start == iota((per_row, ch), 1))
        rh, rl = split(raw_all[col, i, :ch, :])
        acc_ref[...] += mm(sel, rh) + mm(sel, rl)
        dh, dl = split(delayed_ref[:, pl.ds(pl.multiple_of(start, CHUNK), ch)])
        dacc_ref[...] += mm_t(dh, sel) + mm_t(dl, sel)

    index_tables(
        (n_row, nc, rows, cols, width, slots // nc), row, col, ids_ref, dinv_ref, irow_ref, icol_ref, coef_ref, g_ref, want_ref)
    acc_ref[...] = jnp.zeros_like(acc_ref)
    dacc_ref[...] = jnp.zeros_like(dacc_ref)

    @pl.loop(0, nch)
    def _(i):
        @pl.when(i + 2 < nch)
        def _():
            front_copy(i + 2).start()
        front_copy(i).wait()
        pick(i)

        @pl.when(i > 0)
        def _():
            @pl.when(i <= EARLY)
            def _():
                own_step(i - 1)
            pick_rows(i - 1)
    pick_rows(nch - 1)
    piv_all[row, col, :per_row, :] = acc_ref[...]
    for b in range(per_row // LANES):
        piv_all[row, col, per_row + b * nd : per_row + (b + 1) * nd, :] = dacc_ref[:, b * LANES : (b + 1) * LANES]
    diagonal = iota((nd, nd), 0) == iota((nd, nd), 1)
    dest = jnp.sum(jnp.where(diagonal, dest_ref[...].astype(F32), 0.0), axis=1, keepdims=True)
    piv_all[row, col, per_row + per_row // LANES * nd :, :] = jnp.broadcast_to(dest, (nd, wide))

    own_step(EARLY)
    piv_step(y, col, own_piv)

    @pl.loop(1, span + 1)
    def _(s):
        @pl.loop(0, ys * nc)
        def _(q):
            sy, c = q // nc, q % nc
            dist = jnp.abs(c // xs - z) + jnp.abs(c % xs - x) + jnp.abs(sy - y)

            @pl.when(dist == s)
            def _():
                piv_arrived(sy * 2 + k, c)
                piv_step(sy, c, piv_all.at[sy * 2 + k, c])
        own_step(EARLY + s)
    ahead = EARLY + span + 1

    def panel(p, n=1):
        return slice(p * width, (p + n) * width)

    def masks(t):
        at_tile = pl.ds(pl.multiple_of(t * CHUNK, CHUNK), CHUNK)

        @pl.when(t < cols // CHUNK)
        def _():
            ids = iota((slots, CHUNK), 1) + t * CHUNK + col * cols
            hit = jnp.where(icol_ref[:, 1:2].astype(jnp.int32) == ids, 1.0, 0.0)
            ckeep_ref[:, at_tile] = 1.0 - jnp.max(hit, axis=0, keepdims=True)
        ids = iota((CHUNK, slots), 0) + t * CHUNK + row * rows
        hit = jnp.where(irow_ref[0:1, :].astype(jnp.int32) == ids, 1.0, 0.0)
        rkeep_ref[at_tile, :] = 1.0 - jnp.max(hit, axis=1, keepdims=True)

    def gather_square():
        @pl.loop(0, ys * nc)
        def _(q):
            piv_arrived((q // nc) * 2 + 1 - k, q % nc)

        @pl.loop(0, panels - 1)
        def _(p):
            part = pl.ds(pl.multiple_of(p * width, width), width)
            later = pl.ds(pl.multiple_of((p + 1) * width, width), width)
            rowperm[part, :] = one_hot(icol_ref[later, 0:1].astype(jnp.int32) == iota((width, n_row * per_row), 1))

        @pl.loop(0, nc // 2)
        def _(c2):
            block = jnp.concatenate(
                [
                    jnp.concatenate([piv_all[r, c2 * 2 + b, :per_row, :] for b in range(2)], axis=1)
                    for r in range(n_row)
                ],
                axis=0,
            )
            h, l = split(block)
            at_cols = pl.ds(pl.multiple_of(c2 * 2 * wide, 2 * wide), 2 * wide)

            @pl.loop(0, panels - 1)
            def _(p):
                part = pl.ds(pl.multiple_of(p * width, width), width)
                perm = rowperm[part, :]
                a, b = split(mm(perm, h) + mm(perm, l))
                t1h[part, at_cols] = a
                t1l[part, at_cols] = b
        rest = [
            jnp.concatenate(
                [
                    piv_all[r, c, per_row + b * nd : per_row + (b + 1) * nd, :]
                    for r in range(n_row)
                    for b in range(per_row // LANES)
                ],
                axis=1,
            )
            for c in range(nc)
        ]
        h, l = split(jnp.concatenate(rest, axis=0))

        @pl.loop(0, panels - 1)
        def _(p):
            part = pl.ds(pl.multiple_of(p * width, width), width)
            perm = rowperm[part, :]
            a, b = split(mm_t(perm, h) + mm_t(perm, l))
            t1h[part, kraw:] = a
            t1l[part, kraw:] = b

    def dests():
        return jnp.concatenate(
            [piv_all[0, c, per_row + per_row // LANES * nd :, 0:1] for c in range(nc)], axis=0
        ).astype(jnp.int32)

    def square():
        d = dests()

        @pl.loop(0, panels - 1)
        def _(p):
            part = pl.ds(pl.multiple_of(p * width, width), width)
            slot = irow_ref[1:2, part].astype(jnp.int32)
            take = one_hot(slot == iota((kraw, width), 0))
            put = one_hot(d == iota((nc * nd, width), 1) + p * width)
            take = jnp.concatenate([take, put], axis=0)

            @pl.loop(0, panels - 1)
            def _(r):
                rows = pl.ds(pl.multiple_of(r * width, width), width)
                h, l = split(mm(t1h[rows, :], take) + mm(t1l[rows, :], take))
                qh[rows, part] = h
                ql[rows, part] = l

    def dot3(a, b, f):
        return f(a[0], b[0]) + f(a[0], b[1]) + f(a[1], b[0])

    def recur():
        nh[...] = jnp.zeros_like(nh)
        nl[...] = jnp.zeros_like(nl)
        for p in range(panels):
            mine = split(linv_ref[p])
            nh[panel(p), panel(p)], nl[panel(p), panel(p)] = mine
            if p == 0:
                continue
            e, until = p - 1, slice(0, p * width)
            for q in range(p, panels):
                rows = panel(q - 1)
                r = dot3((qh[rows, until], ql[rows, until]), (nh[panel(e), until], nl[panel(e), until]), mm_t)
                rd[rows, panel(e)] = pair_scale(r, coef_ref, panel(e))
            b = dot3(mine, split(rd[panel(p - 1), until]), mm)
            out = dot3(split(-b), (nh[until, until], nl[until, until]), mm)
            nh[panel(p), until], nl[panel(p), until] = split(out)

    def spread():
        step = 2 * wide

        @pl.loop(0, kraw // step)
        def _(t):
            part = pl.ds(pl.multiple_of(t * step, step), step)
            take = one_hot(irow_ref[1:2, :].astype(jnp.int32) == iota((step, slots), 0) + t * step)
            mh[part, :] = mm_t(take, nh[...]).astype(BF16)
            ml[part, :] = mm_t(take, nl[...]).astype(BF16)
        put = one_hot(dests() == iota((nc * nd, slots), 1))
        h = mm_t(put, nh[...]).astype(BF16)
        mh[kraw:, :] = jnp.concatenate([h, mm_t(put, nl[...]).astype(BF16), h], axis=0)

    def chunk_parts(ref, e):
        blocks = [e * sub + b for b in range(sub)]
        a = jnp.concatenate(
            [jnp.concatenate([ref[c, i, :ch, :] for c in range(nc)], axis=1) for i in blocks], axis=0)
        d = jnp.concatenate(
            [
                jnp.concatenate(
                    [ref[c, i, ch + b * nd : ch + (b + 1) * nd, :] for i in blocks for b in range(ch // LANES)], axis=1)
                for c in range(nc)
            ],
            axis=0,
        )
        dh, dl = split(d.T)
        ah, al = split(a)
        return jnp.concatenate([ah, dh, dh, dl], axis=1), ah, al

    def scaled_tile(parts, part):
        return mm(parts[0], mh[:, part]) + mm(parts[1], ml[:, part]) + mm(parts[2], mh[:kraw, part])

    def cols_copy(e):
        rows = pl.ds(pl.multiple_of(row_tile(e, nch // sub, halves) * CHUNK, CHUNK), CHUNK)
        return pltpu.make_async_copy(stage.at[e % 2], cols_out.at[rows, :], out_sem.at[e % 2])

    def eliminate(e):
        @pl.when(e >= 2)
        def _():
            cols_copy(e - 2).wait()
        parts = chunk_parts(raw_all, e)
        for p in range(0, panels, WIDE):
            scaled = scaled_tile(parts, panel(p, WIDE))
            stage[e % 2, :, panel(p, WIDE)] = pair_scale(scaled, coef_ref, panel(p, WIDE))
        cols_copy(e).start()

    def side_copies(e):
        cols = pl.ds(pl.multiple_of(e * CHUNK, CHUNK), CHUNK)
        return (
            pltpu.make_async_copy(stage_h.at[e % 2], hi_out.at[:, cols], hi_sem.at[e % 2]),
            pltpu.make_async_copy(stage_l.at[e % 2], lo_out.at[:, cols], lo_sem.at[e % 2]),
        )

    def eliminate_side(e):
        @pl.when(k != root_k)
        def _():
            @pl.loop(0, nc)
            def _(c):
                for b in range(sub):
                    col_arrived(c, e * sub + b)

        @pl.when(is_root)
        def _():
            @pl.loop(0, nc)
            def _(c):
                for b in range(sub):
                    ref = col_raw.at[c, e * sub + b]
                    pltpu.make_async_copy(ref, ref, root_sem.at[c, e * sub + b]).wait()

        @pl.when(e >= 2)
        def _():
            for copy in side_copies(e - 2):
                copy.wait()
        parts = chunk_parts(col_raw, e)
        for p in range(0, panels, WIDE):
            stage_h[e % 2, panel(p, WIDE), :], stage_l[e % 2, panel(p, WIDE), :] = split(
                scaled_tile(parts, panel(p, WIDE)).T)
        for copy in side_copies(e):
            copy.start()

    first = max(reach - 1, 3)
    side_lag = reach - 1 + ys
    work = [gather_square, square, recur, spread]

    @pl.loop(0, nch + max(first, side_lag))
    def _(s):
        own_step(s + ahead)

        @pl.loop(0, nc)
        def _(c):
            dist = jnp.abs(c // xs - z) + jnp.abs(c % xs - x)
            i = s - (dist - 1)

            @pl.when((dist >= 1) & (i >= 0) & (i < nch))
            def _():
                raw_arrived(c, i)
                raw_step(c, i, raw_all.at[c, i])

        @pl.when(at_root_core & (y != root_y))
        def _():
            @pl.loop(0, nc)
            def _(c):
                dist = jnp.abs(c // xs - z) + jnp.abs(c % xs - x)
                j, mine = side_of(s - (jnp.maximum(dist, 1) - 1) - jnp.abs(y - root_y))

                @pl.when(mine)
                def _():
                    col_arrived(c, j)
                    src = col_raw.at[c, j]

                    @pl.when((y > root_y) & (y + 1 < ys))
                    def _():
                        col_copy(4, c, j, src).start()

                    @pl.when((y < root_y) & (y >= 1))
                    def _():
                        col_copy(5, c, j, src).start()
                    col_copy(6, c, j, src).start()

        for n, piece in enumerate(work):
            pl.when(s == n)(piece)

        @pl.when(s < rows // CHUNK)
        def _():
            masks(s)

        i = s - first

        @pl.when((i >= 0) & (i < nch) & (i % sub == sub - 1))
        def _():
            eliminate(i // sub)
        j, mine = side_of(s - side_lag)

        @pl.when(mine & (j % sub == sub - 1))
        def _():
            eliminate_side(j // sub)

    for e in range(max(nch // sub - 2, 0), nch // sub):
        cols_copy(e).wait()
    for e in range(max(hch // sub - 2, 0), hch // sub):
        for copy in side_copies(e):
            copy.wait()

    @pl.loop(0, ys * nc)
    def _(q):
        sy, c = q // nc, q % nc
        for way, cond in piv_ways(sy, c):
            @pl.when(cond)
            def _(way=way):
                piv_copy(way, sy, c, own_piv).wait_send()
        piv_copy(6, sy, c, own_piv).wait_send()

    def sent(ref, sem):
        pltpu.make_async_copy(ref, ref, sem).wait()

    @pl.loop(0, nc)
    def _(c):
        for way, cond, line, part in raw_ways(c):
            @pl.when(cond & line)
            def _(way=way):
                sent(raw_all.at[c], raw_send.at[way, c])

            @pl.when(cond & jnp.logical_not(line))
            def _(way=way, part=part):
                sent(raw_all.at[c, :, part], raw_send.at[way, c])

        @pl.when(is_root | (at_root_core & (y > root_y)))
        def _():
            @pl.when(y + 1 < ys)
            def _():
                sent(col_raw.at[c], col_send.at[0, c])

        @pl.when(is_root | (at_root_core & (y < root_y)))
        def _():
            @pl.when(y >= 1)
            def _():
                sent(col_raw.at[c], col_send.at[1, c])

        @pl.when(at_root_core)
        def _():
            sent(col_raw.at[c], col_send.at[2, c])


def pair_scale(scaled, coef_ref, part):
    width = scaled.shape[1]
    return (
        scaled * coef_ref[0:1, part]
        + pltpu.roll(scaled, width - 1, 1) * coef_ref[1:2, part]
        + pltpu.roll(scaled, 1, 1) * coef_ref[2:3, part]
    )


def gather(front, delayed, dest, ids, dinv, linv):
    n_col = lax.axis_size("col")
    n_row = lax.axis_size("row")
    rows, cols = front.shape
    nd = delayed.shape[0]
    panels, width, _ = linv.shape
    slots = panels * width
    per_col = slots // n_col
    per_row = slots // n_row
    wide = (per_col + LANES - 1) // LANES * LANES
    nch = rows // COMM
    high = COMM + nd * (COMM // LANES)
    piv_high = per_row + nd * (per_row // LANES) + nd
    halves = rows // cols
    ys = n_row // 2
    xs = ys if n_col % ys == 0 else 1
    zs = n_col // xs
    hch = nch // halves
    x_rows = (high + 47) // 48 * 8
    kraw = n_col * wide
    kall = kraw + n_col * nd
    early = slots - width
    vmem = pl.BlockSpec(memory_space=pltpu.VMEM)
    hbm = pl.BlockSpec(memory_space=pl.ANY)
    dma = pltpu.SemaphoreType.DMA
    return pl.pallas_call(
        functools.partial(gather_kernel, (zs, xs, ys, halves, per_row, nd, x_rows)),
        out_shape=(
            jax.ShapeDtypeStruct((rows, slots), F32),
            jax.ShapeDtypeStruct((slots, cols), BF16),
            jax.ShapeDtypeStruct((slots, cols), BF16),
            jax.ShapeDtypeStruct((rows, 1), F32),
            jax.ShapeDtypeStruct((1, cols), F32),
        ),
        in_specs=[hbm] + [vmem] * 5,
        out_specs=(hbm, hbm, hbm, vmem, vmem),
        scratch_shapes=[
            pltpu.VMEM((8, slots), F32),
            pltpu.VMEM((slots, 8), F32),
            pltpu.VMEM((8, slots), F32),
            pltpu.VMEM((cols, wide), BF16),
            pltpu.VMEM((per_row, 1), F32),
            pltpu.VMEM((per_row, wide), F32),
            pltpu.VMEM((nd, per_row), F32),
            pltpu.VMEM((3, CHUNK, cols), F32),
            pltpu.VMEM((n_col, nch, high, wide), F32),
            pltpu.VMEM((n_col, hch, high, wide), F32),
            pltpu.VMEM((n_row, n_col, piv_high, wide), F32),
            pltpu.VMEM((early, slots), BF16),
            pltpu.VMEM((early, kall), BF16),
            pltpu.VMEM((early, kall), BF16),
            pltpu.VMEM((early, early), BF16),
            pltpu.VMEM((early, early), BF16),
            pltpu.VMEM((slots, slots), BF16),
            pltpu.VMEM((slots, slots), BF16),
            pltpu.VMEM((early, early), F32),
            pltpu.VMEM((kraw + 3 * n_col * nd, slots), BF16),
            pltpu.VMEM((kraw, slots), BF16),
            pltpu.VMEM((2, CHUNK, slots), F32),
            pltpu.VMEM((2, slots, CHUNK), BF16),
            pltpu.VMEM((2, slots, CHUNK), BF16),
            dma((3,)),
            dma((n_col, hch)),
            dma((n_col, nch, 2)),
            dma((4, n_col)),
            dma((n_col, hch)),
            dma((3, n_col)),
            dma((n_row, n_col)),
            dma((7, ys * n_col)),
            dma((2,)),
            dma((2,)),
            dma((2,)),
        ],
        compiler_params=pltpu.CompilerParams(
            collective_id=0, has_side_effects=True, vmem_limit_bytes=VMEM_LIMIT
        ),
    )(front, delayed, dest, ids, dinv, linv)


def trailing_kernel(c_ref, hi_ref, lo_ref, front_ref, rkeep_ref, ckeep_ref, out_ref, factor_ref):
    columns = c_ref[...]
    factor_ref[...] = columns
    hi, lo = split(columns)
    bh = hi_ref[...]
    acc = mm(hi, bh) + mm(hi, lo_ref[...]) + mm(lo, bh)
    keep = (rkeep_ref[...] > 0.0) & (ckeep_ref[...] > 0.0)
    out_ref[...] = jnp.where(keep, front_ref[...] - acc, 0.0)


def update(columns, side_hi, side_lo, front, row_keep, col_keep):
    rows, cols = front.shape
    slots = columns.shape[1]
    tile = 256
    return pl.pallas_call(
        trailing_kernel,
        grid=(rows // tile,),
        in_specs=[
            pl.BlockSpec((tile, slots), lambda i: (i, 0)),
            pl.BlockSpec((slots, cols), lambda i: (0, 0)),
            pl.BlockSpec((slots, cols), lambda i: (0, 0)),
            pl.BlockSpec((tile, cols), lambda i: (i, 0)),
            pl.BlockSpec((tile, 1), lambda i: (i, 0)),
            pl.BlockSpec((1, cols), lambda i: (0, 0)),
        ],
        out_specs=(
            pl.BlockSpec((tile, cols), lambda i: (i, 0)),
            pl.BlockSpec((tile, slots), lambda i: (i, 0)),
        ),
        out_shape=(
            jax.ShapeDtypeStruct((rows, cols), F32),
            jax.ShapeDtypeStruct((rows, slots), F32),
        ),
        compiler_params=pltpu.CompilerParams(dimension_semantics=("arbitrary",), vmem_limit_bytes=VMEM_LIMIT),
    )(columns, side_hi, side_lo, front, row_keep, col_keep)


def body(front, delayed, dest, pivots, pair_flags, linv, dinv_diag, dinv_off):
    ids = jnp.stack([pivots, pair_flags])
    dinv = jnp.stack([dinv_diag, dinv_off])
    columns, side_hi, side_lo, row_keep, col_keep = gather(front, delayed, dest[None, :], ids, dinv, linv)
    trailing, factor = update(columns, side_hi, side_lo, front, row_keep, col_keep)
    return (trailing, factor)


def solution(mesh):
    return jax.shard_map(
        body,
        mesh=mesh,
        in_specs=(P("row", "col"), P("col", "row"), P("col"), P(), P(), P(), P(), P()),
        out_specs=(P("row", "col"), P("row", None)),
        check_vma=False,
    )
```

```python
import functools

import jax
import jax.numpy as jnp
from jax import lax
from jax.experimental import pallas as pl
from jax.experimental.pallas import tpu as pltpu
from jax.sharding import PartitionSpec as P

MESH = pl.DeviceIdType.MESH
VMEM_LIMIT = 66_800_000
F32 = jnp.float32
BF16 = jnp.bfloat16
CHUNK = 256
COMM = 256
EARLY = 4
WIDE = 4
LANES = 128


def split(a):
    hi = a.astype(BF16)
    return hi, (a - hi.astype(F32)).astype(BF16)


def mm(a, b):
    return lax.dot_general(a, b, (((1,), (0,)), ((), ())), preferred_element_type=F32)


def mm_t(a, b):
    return lax.dot_general(a, b, (((1,), (1,)), ((), ())), preferred_element_type=F32)


def iota(shape, dim):
    return lax.broadcasted_iota(jnp.int32, shape, dim)


def one_hot(mask):
    return jnp.where(mask, 1.0, 0.0).astype(BF16)


def owner_of(ids, block, n):
    total = jnp.zeros(ids.shape, F32)
    for c in range(1, n):
        total += jnp.where(ids >= c * block, 1.0, 0.0)
    return total


def rank_of(owner_row, owner_col):
    slots = owner_row.shape[1]
    total = jnp.zeros((1, slots), F32)
    for t in range(slots // CHUNK):
        here = slice(t * CHUNK, (t + 1) * CHUNK)
        before = iota((CHUNK, slots), 0) + t * CHUNK < iota((CHUNK, slots), 1)
        same = owner_col[here, :] == owner_row
        total += jnp.sum(jnp.where(before & same, 1.0, 0.0), axis=0, keepdims=True)
    return total


def turned(row):
    return jnp.broadcast_to(row, (8, row.shape[1])).T[:, 0:1]


def col_tables(dims, col_id, slot_refs, irow_ref, icol_ref, g_ref):
    _, n_col, _, cols, _, per_col = dims
    piv_ref = slot_refs[0]
    slots = piv_ref.shape[1]
    wide = g_ref.shape[1]
    piv = piv_ref[...].astype(F32)
    col_owner = owner_of(piv, cols, n_col)
    col_pos = col_owner * wide + rank_of(col_owner, turned(col_owner))
    piv_col = turned(piv)
    irow_ref[...] = jnp.zeros_like(irow_ref)
    irow_ref[0:1, :] = piv
    irow_ref[1:2, :] = col_pos
    icol_ref[...] = jnp.zeros_like(icol_ref)
    icol_ref[:, 1:2] = piv_col
    mine = turned(col_pos) - (col_id * wide).astype(F32) == iota((slots, wide), 1).astype(F32)
    want_col = jnp.sum(jnp.where(mine, piv_col - (col_id * cols).astype(F32), 0.0), axis=0, keepdims=True)
    want_col = jnp.where(iota((1, wide), 1) < per_col, want_col, -1.0)
    g_ref[...] = one_hot(iota((cols, wide), 0).astype(F32) == want_col)


def row_tables(dims, row_id, slot_refs, icol_ref, coef_ref, want_ref):
    n_row, _, rows, _, width, _ = dims
    piv_ref, flag_ref, diag_ref, off_ref = slot_refs
    slots = piv_ref.shape[1]
    per_row = want_ref.shape[0]
    piv = piv_ref[...].astype(F32)
    row_owner = owner_of(piv, rows, n_row)
    row_pos = row_owner * per_row + rank_of(row_owner, turned(row_owner))
    icol_ref[:, 0:1] = turned(row_pos)
    mine = row_pos - (row_id * per_row).astype(F32) == iota((per_row, slots), 0).astype(F32)
    want_ref[...] = jnp.sum(jnp.where(mine, piv - (row_id * rows).astype(F32), 0.0), axis=1, keepdims=True)

    slot = iota((1, slots), 1) % width
    coupled = flag_ref[...].astype(F32) * off_ref[...]
    coef_ref[...] = jnp.zeros_like(coef_ref)
    coef_ref[0:1, :] = diag_ref[...]
    coef_ref[1:2, :] = jnp.where(slot == width - 1, 0.0, coupled)
    coef_ref[2:3, :] = jnp.where(slot == 0, 0.0, pltpu.roll(jnp.broadcast_to(coupled, (8, slots)), 1, 1)[0:1, :])


def row_tile(i, tiles, halves):
    return i % halves * (tiles // halves) + i // halves


def gather_kernel(
    dims, front_ref, delayed_ref, dest_ref, piv_ref, flag_ref, diag_ref, off_ref, linv_ref,
    cols_out, hi_out, lo_out, rkeep_ref, ckeep_ref,
    irow_ref, icol_ref, coef_ref, g_ref, want_ref, acc_ref, dacc_ref, fbuf,
    raw_all, col_raw, piv_all, t1h, t1l, qh, ql, nh, nl, rd, mh, ml, stage, stage_h, stage_l,
    front_sem, root_sem, raw_recv, raw_send, col_recv, col_send, piv_recv, piv_send, out_sem, hi_sem, lo_sem,
):
    zs, xs, ys, halves, per_row, nd, x_rows = dims
    nc, n_row = zs * xs, ys * 2
    nch, high, wide = raw_all.shape[1:]
    rows, cols = front_ref.shape
    hch = nch // halves
    panels, width, _ = linv_ref.shape
    slots = panels * width
    ch = COMM
    sub = CHUNK // COMM
    z_part, x_part = pl.ds(0, high - x_rows), pl.ds(high - x_rows, x_rows)
    kraw = nc * wide
    row, col = lax.axis_index("row"), lax.axis_index("col")
    y, k = row // 2, row % 2
    z, x = col // xs, col % xs
    root = col // halves
    half = col % halves
    root_y, root_k = root // 2, root % 2
    is_root = row == root
    at_root_core = k == root_k
    reach = zs + xs - 2
    span = reach + ys - 1

    def at(y_, k_, z_, x_):
        return (y_ * 2 + k_, z_ * xs + x_)

    links = [
        (z + 1 < zs, at(y, k, z + 1, x)),
        (z >= 1, at(y, k, z - 1, x)),
        (x + 1 < xs, at(y, k, z, x + 1)),
        (x >= 1, at(y, k, z, x - 1)),
        (y + 1 < ys, at(y + 1, k, z, x)),
        (y >= 1, at(y - 1, k, z, x)),
        (None, at(y, 1 - k, z, x)),
    ]

    for i in range(min(2, nch)):
        tile = pl.ds(row_tile(i, nch, halves) * CHUNK, CHUNK)
        pltpu.make_async_copy(front_ref.at[tile, :], fbuf.at[i], front_sem.at[i]).start()

    barrier = pltpu.get_barrier_semaphore()
    peers = 1
    for cond, dev in links:
        if cond is None:
            pl.semaphore_signal(barrier, inc=1, device_id=dev, device_id_type=MESH)
        else:
            peers = peers + jnp.where(cond, 1, 0)

            @pl.when(cond)
            def _(dev=dev):
                pl.semaphore_signal(barrier, inc=1, device_id=dev, device_id_type=MESH)

    def remote(way, src, dst, send, recv):
        return pltpu.make_async_remote_copy(
            src_ref=src, dst_ref=dst, send_sem=send, recv_sem=recv, device_id=links[way][1], device_id_type=MESH)

    def piv_ways(sy, c):
        zc, xc = c // xs, c % xs
        same_y = sy == y
        same_x = xc == x
        return [
            (0, (z + 1 < zs) & (zc <= z) & same_x & same_y),
            (1, (z >= 1) & (zc >= z) & same_x & same_y),
            (2, (x + 1 < xs) & (xc <= x) & same_y),
            (3, (x >= 1) & (xc >= x) & same_y),
            (4, (y + 1 < ys) & (sy <= y)),
            (5, (y >= 1) & (sy >= y)),
        ]

    def piv_copy(way, sy, c, src):
        s = sy * 2 + k
        return remote(way, src, piv_all.at[s, c], piv_send.at[way, sy * nc + c], piv_recv.at[s, c])

    def piv_arrived(s, c):
        pltpu.make_async_copy(piv_all.at[s, c], piv_all.at[s, c], piv_recv.at[s, c]).wait()

    def piv_step(sy, c, src):
        for way, cond in piv_ways(sy, c):
            @pl.when(cond)
            def _(way=way):
                piv_copy(way, sy, c, src).start()
        piv_copy(6, sy, c, src).start()

    def raw_ways(c):
        zc, xc = c // xs, c % xs
        same_x, same_z = xc == x, zc == z
        return [
            (0, (z + 1 < zs) & (zc <= z), same_x, x_part),
            (1, (z >= 1) & (zc >= z), same_x, x_part),
            (2, (x + 1 < xs) & (xc <= x), same_z, z_part),
            (3, (x >= 1) & (xc >= x), same_z, z_part),
        ]

    def side_of(i):
        e = i // sub
        return e // halves * sub + i % sub, (i >= 0) & (i < nch) & (e % halves == half)

    def raw_arrived(c, i):
        line = (c // xs == z) | (c % xs == x)
        whole = raw_all.at[c, i]

        @pl.when(line)
        def _():
            pltpu.make_async_copy(whole, whole, raw_recv.at[c, i, 0]).wait()

        @pl.when(jnp.logical_not(line))
        def _():
            for n, part in enumerate((z_part, x_part)):
                ref = raw_all.at[c, i, part]
                pltpu.make_async_copy(ref, ref, raw_recv.at[c, i, n]).wait()

    def col_copy(way, c, j, src):
        return remote(way, src, col_raw.at[c, j], col_send.at[way - 4, c], col_recv.at[c, j])

    def raw_step(c, i, src):
        for way, cond, line, part in raw_ways(c):
            @pl.when(cond & line)
            def _(way=way):
                remote(way, src, raw_all.at[c, i], raw_send.at[way, c], raw_recv.at[c, i, 0]).start()

            @pl.when(cond & jnp.logical_not(line))
            def _(way=way, part=part):
                remote(
                    way, src.at[part], raw_all.at[c, i, part],
                    raw_send.at[way, c], raw_recv.at[c, i, 1 if way < 2 else 0]).start()
        j, mine = side_of(i)

        @pl.when(is_root & mine)
        def _():
            @pl.when(y + 1 < ys)
            def _():
                col_copy(4, c, j, src).start()

            @pl.when(y >= 1)
            def _():
                col_copy(5, c, j, src).start()
            col_copy(6, c, j, src).start()
            pltpu.make_async_copy(src, col_raw.at[c, j], root_sem.at[c, j]).start()

    def col_arrived(c, j):
        pltpu.make_async_copy(col_raw.at[c, j], col_raw.at[c, j], col_recv.at[c, j]).wait()

    own_piv = piv_all.at[row, col]

    def own_step(i):
        @pl.when(i < nch)
        def _():
            raw_step(col, i, raw_all.at[col, i])

    def front_copy(i):
        tile = pl.ds(pl.multiple_of(row_tile(i, nch, halves) * CHUNK, CHUNK), CHUNK)
        return pltpu.make_async_copy(front_ref.at[tile, :], fbuf.at[i % 3], front_sem.at[i % 3])

    def pick(i):
        hi, lo = split(fbuf[i % 3])
        g = g_ref[...]
        raw_all[col, i, :ch, :] = mm(hi, g) + mm(lo, g)
        start = row_tile(i, nch, halves) * CHUNK
        for t in range(ch // LANES):
            part = pl.ds(pl.multiple_of(start + t * LANES, LANES), LANES)
            raw_all[col, i, ch + t * nd : ch + (t + 1) * nd, :] = delayed_ref[:, part]

    def pick_rows(i):
        start = row_tile(i, nch, halves) * CHUNK
        sel = one_hot(want_ref[...].astype(jnp.int32) - start == iota((per_row, ch), 1))
        rh, rl = split(raw_all[col, i, :ch, :])
        acc_ref[...] += mm(sel, rh) + mm(sel, rl)
        dh, dl = split(delayed_ref[:, pl.ds(pl.multiple_of(start, CHUNK), ch)])
        dacc_ref[...] += mm_t(dh, sel) + mm_t(dl, sel)

    tables = (n_row, nc, rows, cols, width, slots // nc)
    slot_refs = (piv_ref, flag_ref, diag_ref, off_ref)
    col_tables(tables, col, slot_refs, irow_ref, icol_ref, g_ref)
    pl.semaphore_wait(barrier, peers)
    acc_ref[...] = jnp.zeros_like(acc_ref)
    dacc_ref[...] = jnp.zeros_like(dacc_ref)

    @pl.loop(0, nch)
    def _(i):
        @pl.when(i + 2 < nch)
        def _():
            front_copy(i + 2).start()
        front_copy(i).wait()
        pick(i)

        @pl.when(i > 0)
        def _():
            @pl.when(i <= EARLY)
            def _():
                own_step(i - 1)

            @pl.when(i == 1)
            def _():
                row_tables(tables, row, slot_refs, icol_ref, coef_ref, want_ref)
            pick_rows(i - 1)
    pick_rows(nch - 1)
    piv_all[row, col, :per_row, :] = acc_ref[...]
    for b in range(per_row // LANES):
        piv_all[row, col, per_row + b * nd : per_row + (b + 1) * nd, :] = dacc_ref[:, b * LANES : (b + 1) * LANES]
    diagonal = iota((nd, nd), 0) == iota((nd, nd), 1)
    dest = jnp.sum(jnp.where(diagonal, dest_ref[...].astype(F32), 0.0), axis=1, keepdims=True)
    piv_all[row, col, per_row + per_row // LANES * nd :, :] = jnp.broadcast_to(dest, (nd, wide))

    own_step(EARLY)
    piv_step(y, col, own_piv)

    @pl.loop(1, span + 1)
    def _(s):
        @pl.loop(0, ys * nc)
        def _(q):
            sy, c = q // nc, q % nc
            dist = jnp.abs(c // xs - z) + jnp.abs(c % xs - x) + jnp.abs(sy - y)

            @pl.when(dist == s)
            def _():
                piv_arrived(sy * 2 + k, c)
                piv_step(sy, c, piv_all.at[sy * 2 + k, c])
        own_step(EARLY + s)
    ahead = EARLY + span + 1

    def panel(p, n=1):
        return slice(p * width, (p + n) * width)

    def masks(t):
        at_tile = pl.ds(pl.multiple_of(t * CHUNK, CHUNK), CHUNK)

        @pl.when(t < cols // CHUNK)
        def _():
            ids = iota((slots, CHUNK), 1) + t * CHUNK + col * cols
            hit = jnp.where(icol_ref[:, 1:2].astype(jnp.int32) == ids, 1.0, 0.0)
            ckeep_ref[:, at_tile] = 1.0 - jnp.max(hit, axis=0, keepdims=True)
        ids = iota((CHUNK, slots), 0) + t * CHUNK + row * rows
        hit = jnp.where(irow_ref[0:1, :].astype(jnp.int32) == ids, 1.0, 0.0)
        rkeep_ref[at_tile, :] = 1.0 - jnp.max(hit, axis=1, keepdims=True)

    def gather_square():
        @pl.loop(0, ys * nc)
        def _(q):
            piv_arrived((q // nc) * 2 + 1 - k, q % nc)

        @pl.loop(0, panels - 1)
        def _(p):
            part = pl.ds(pl.multiple_of(p * width, width), width)
            later = pl.ds(pl.multiple_of((p + 1) * width, width), width)
            mh[part, :] = one_hot(icol_ref[later, 0:1].astype(jnp.int32) == iota((width, n_row * per_row), 1))

        @pl.loop(0, nc // 2)
        def _(c2):
            block = jnp.concatenate(
                [
                    jnp.concatenate([piv_all[r, c2 * 2 + b, :per_row, :] for b in range(2)], axis=1)
                    for r in range(n_row)
                ],
                axis=0,
            )
            h, l = split(block)
            at_cols = pl.ds(pl.multiple_of(c2 * 2 * wide, 2 * wide), 2 * wide)

            @pl.loop(0, panels - 1)
            def _(p):
                part = pl.ds(pl.multiple_of(p * width, width), width)
                perm = mh[part, :]
                a, b = split(mm(perm, h) + mm(perm, l))
                t1h[part, at_cols] = a
                t1l[part, at_cols] = b
        rest = [
            jnp.concatenate(
                [
                    piv_all[r, c, per_row + b * nd : per_row + (b + 1) * nd, :]
                    for r in range(n_row)
                    for b in range(per_row // LANES)
                ],
                axis=1,
            )
            for c in range(nc)
        ]
        h, l = split(jnp.concatenate(rest, axis=0))

        @pl.loop(0, panels - 1)
        def _(p):
            part = pl.ds(pl.multiple_of(p * width, width), width)
            perm = mh[part, :]
            a, b = split(mm_t(perm, h) + mm_t(perm, l))
            t1h[part, kraw:] = a
            t1l[part, kraw:] = b

    def dests():
        return jnp.concatenate(
            [piv_all[0, c, per_row + per_row // LANES * nd :, 0:1] for c in range(nc)], axis=0
        ).astype(jnp.int32)

    def square():
        d = dests()

        @pl.loop(0, panels - 1)
        def _(p):
            part = pl.ds(pl.multiple_of(p * width, width), width)
            slot = irow_ref[1:2, part].astype(jnp.int32)
            take = one_hot(slot == iota((kraw, width), 0))
            put = one_hot(d == iota((nc * nd, width), 1) + p * width)
            take = jnp.concatenate([take, put], axis=0)

            @pl.loop(0, panels - 1)
            def _(r):
                rows = pl.ds(pl.multiple_of(r * width, width), width)
                h, l = split(mm(t1h[rows, :], take) + mm(t1l[rows, :], take))
                qh[rows, part] = h
                ql[rows, part] = l

    def dot3(a, b, f):
        return f(a[0], b[0]) + f(a[0], b[1]) + f(a[1], b[0])

    def recur():
        nh[...] = jnp.zeros_like(nh)
        nl[...] = jnp.zeros_like(nl)
        for p in range(panels):
            mine = split(linv_ref[p])
            nh[panel(p), panel(p)], nl[panel(p), panel(p)] = mine
            if p == 0:
                continue
            e, until = p - 1, slice(0, p * width)
            for q in range(p, panels):
                rows = panel(q - 1)
                r = dot3((qh[rows, until], ql[rows, until]), (nh[panel(e), until], nl[panel(e), until]), mm_t)
                rd[rows, panel(e)] = pair_scale(r, coef_ref, panel(e))
            b = dot3(mine, split(rd[panel(p - 1), until]), mm)
            out = dot3(split(-b), (nh[until, until], nl[until, until]), mm)
            nh[panel(p), until], nl[panel(p), until] = split(out)

    def spread():
        step = 2 * wide

        @pl.loop(0, kraw // step)
        def _(t):
            part = pl.ds(pl.multiple_of(t * step, step), step)
            take = one_hot(irow_ref[1:2, :].astype(jnp.int32) == iota((step, slots), 0) + t * step)
            mh[part, :] = mm_t(take, nh[...]).astype(BF16)
            ml[part, :] = mm_t(take, nl[...]).astype(BF16)
        put = one_hot(dests() == iota((nc * nd, slots), 1))
        h = mm_t(put, nh[...]).astype(BF16)
        mh[kraw:, :] = jnp.concatenate([h, mm_t(put, nl[...]).astype(BF16), h], axis=0)

    def chunk_parts(ref, e):
        blocks = [e * sub + b for b in range(sub)]
        a = jnp.concatenate(
            [jnp.concatenate([ref[c, i, :ch, :] for c in range(nc)], axis=1) for i in blocks], axis=0)
        d = jnp.concatenate(
            [
                jnp.concatenate(
                    [ref[c, i, ch + b * nd : ch + (b + 1) * nd, :] for i in blocks for b in range(ch // LANES)], axis=1)
                for c in range(nc)
            ],
            axis=0,
        )
        dh, dl = split(d.T)
        ah, al = split(a)
        return jnp.concatenate([ah, dh, dh, dl], axis=1), ah, al

    def scaled_tile(parts, part):
        return mm(parts[0], mh[:, part]) + mm(parts[1], ml[:, part]) + mm(parts[2], mh[:kraw, part])

    def cols_copy(e):
        rows = pl.ds(pl.multiple_of(row_tile(e, nch // sub, halves) * CHUNK, CHUNK), CHUNK)
        return pltpu.make_async_copy(stage.at[e % 2], cols_out.at[rows, :], out_sem.at[e % 2])

    def eliminate(e):
        @pl.when(e >= 2)
        def _():
            cols_copy(e - 2).wait()
        parts = chunk_parts(raw_all, e)
        for p in range(0, panels, WIDE):
            scaled = scaled_tile(parts, panel(p, WIDE))
            stage[e % 2, :, panel(p, WIDE)] = pair_scale(scaled, coef_ref, panel(p, WIDE))
        cols_copy(e).start()

    def side_copies(e):
        cols = pl.ds(pl.multiple_of(e * CHUNK, CHUNK), CHUNK)
        return (
            pltpu.make_async_copy(stage_h.at[e % 2], hi_out.at[:, cols], hi_sem.at[e % 2]),
            pltpu.make_async_copy(stage_l.at[e % 2], lo_out.at[:, cols], lo_sem.at[e % 2]),
        )

    def eliminate_side(e):
        @pl.when(k != root_k)
        def _():
            @pl.loop(0, nc)
            def _(c):
                for b in range(sub):
                    col_arrived(c, e * sub + b)

        @pl.when(is_root)
        def _():
            @pl.loop(0, nc)
            def _(c):
                for b in range(sub):
                    ref = col_raw.at[c, e * sub + b]
                    pltpu.make_async_copy(ref, ref, root_sem.at[c, e * sub + b]).wait()

        @pl.when(e >= 2)
        def _():
            for copy in side_copies(e - 2):
                copy.wait()
        parts = chunk_parts(col_raw, e)
        for p in range(0, panels, WIDE):
            stage_h[e % 2, panel(p, WIDE), :], stage_l[e % 2, panel(p, WIDE), :] = split(
                scaled_tile(parts, panel(p, WIDE)).T)
        for copy in side_copies(e):
            copy.start()

    def piv_drain():
        @pl.loop(0, ys * nc)
        def _(q):
            sy, c = q // nc, q % nc
            for way, cond in piv_ways(sy, c):
                @pl.when(cond)
                def _(way=way):
                    piv_copy(way, sy, c, own_piv).wait_send()
            piv_copy(6, sy, c, own_piv).wait_send()

    first = max(reach - 1, 3)
    side_lag = reach - 2 + ys
    work = [gather_square, square, recur, spread]

    @pl.loop(0, nch + max(first, side_lag))
    def _(s):
        own_step(s + ahead)

        @pl.loop(0, nc)
        def _(c):
            dist = jnp.abs(c // xs - z) + jnp.abs(c % xs - x)
            i = s - (dist - 1)

            @pl.when((dist >= 1) & (i >= 0) & (i < nch))
            def _():
                raw_arrived(c, i)
                raw_step(c, i, raw_all.at[c, i])

        @pl.when(at_root_core & (y != root_y))
        def _():
            @pl.loop(0, nc)
            def _(c):
                dist = jnp.abs(c // xs - z) + jnp.abs(c % xs - x)
                j, mine = side_of(s - (jnp.maximum(dist, 1) - 1) - jnp.abs(y - root_y))

                @pl.when(mine)
                def _():
                    col_arrived(c, j)
                    src = col_raw.at[c, j]

                    @pl.when((y > root_y) & (y + 1 < ys))
                    def _():
                        col_copy(4, c, j, src).start()

                    @pl.when((y < root_y) & (y >= 1))
                    def _():
                        col_copy(5, c, j, src).start()
                    col_copy(6, c, j, src).start()

        for n, piece in enumerate(work):
            pl.when(s == n)(piece)

        @pl.when(s < rows // CHUNK)
        def _():
            masks(s)

        pl.when(s == len(work))(piv_drain)

        i = s - first

        @pl.when((i >= 0) & (i < nch) & (i % sub == sub - 1))
        def _():
            eliminate(i // sub)
        j, mine = side_of(s - side_lag)

        @pl.when(mine & (j % sub == sub - 1))
        def _():
            eliminate_side(j // sub)

    for e in range(max(nch // sub - 2, 0), nch // sub):
        cols_copy(e).wait()
    for e in range(max(hch // sub - 2, 0), hch // sub):
        for copy in side_copies(e):
            copy.wait()

    def sent(ref, sem):
        pltpu.make_async_copy(ref, ref, sem).wait()

    @pl.loop(0, nc)
    def _(c):
        for way, cond, line, part in raw_ways(c):
            @pl.when(cond & line)
            def _(way=way):
                sent(raw_all.at[c], raw_send.at[way, c])

            @pl.when(cond & jnp.logical_not(line))
            def _(way=way, part=part):
                sent(raw_all.at[c, :, part], raw_send.at[way, c])

        @pl.when(is_root | (at_root_core & (y > root_y)))
        def _():
            @pl.when(y + 1 < ys)
            def _():
                sent(col_raw.at[c], col_send.at[0, c])

        @pl.when(is_root | (at_root_core & (y < root_y)))
        def _():
            @pl.when(y >= 1)
            def _():
                sent(col_raw.at[c], col_send.at[1, c])

        @pl.when(at_root_core)
        def _():
            sent(col_raw.at[c], col_send.at[2, c])


def pair_scale(scaled, coef_ref, part):
    width = scaled.shape[1]
    return (
        scaled * coef_ref[0:1, part]
        + pltpu.roll(scaled, width - 1, 1) * coef_ref[1:2, part]
        + pltpu.roll(scaled, 1, 1) * coef_ref[2:3, part]
    )


def gather(front, delayed, dest, pivots, flags, diag, off, linv):
    n_col = lax.axis_size("col")
    n_row = lax.axis_size("row")
    rows, cols = front.shape
    nd = delayed.shape[0]
    panels, width, _ = linv.shape
    slots = panels * width
    per_col = slots // n_col
    per_row = slots // n_row
    wide = (per_col + LANES - 1) // LANES * LANES
    nch = rows // COMM
    high = COMM + nd * (COMM // LANES)
    piv_high = per_row + nd * (per_row // LANES) + nd
    halves = rows // cols
    ys = n_row // 2
    xs = ys if n_col % ys == 0 else 1
    zs = n_col // xs
    hch = nch // halves
    x_rows = (high + 47) // 48 * 8
    kraw = n_col * wide
    kall = kraw + n_col * nd
    early = slots - width
    vmem = pl.BlockSpec(memory_space=pltpu.VMEM)
    hbm = pl.BlockSpec(memory_space=pl.ANY)
    dma = pltpu.SemaphoreType.DMA
    return pl.pallas_call(
        functools.partial(gather_kernel, (zs, xs, ys, halves, per_row, nd, x_rows)),
        out_shape=(
            jax.ShapeDtypeStruct((rows, slots), F32),
            jax.ShapeDtypeStruct((slots, cols), BF16),
            jax.ShapeDtypeStruct((slots, cols), BF16),
            jax.ShapeDtypeStruct((rows, 1), F32),
            jax.ShapeDtypeStruct((1, cols), F32),
        ),
        in_specs=[hbm] + [vmem] * 7,
        out_specs=(hbm, hbm, hbm, vmem, vmem),
        scratch_shapes=[
            pltpu.VMEM((8, slots), F32),
            pltpu.VMEM((slots, 8), F32),
            pltpu.VMEM((8, slots), F32),
            pltpu.VMEM((cols, wide), BF16),
            pltpu.VMEM((per_row, 1), F32),
            pltpu.VMEM((per_row, wide), F32),
            pltpu.VMEM((nd, per_row), F32),
            pltpu.VMEM((3, CHUNK, cols), F32),
            pltpu.VMEM((n_col, nch, high, wide), F32),
            pltpu.VMEM((n_col, hch, high, wide), F32),
            pltpu.VMEM((n_row, n_col, piv_high, wide), F32),
            pltpu.VMEM((early, kall), BF16),
            pltpu.VMEM((early, kall), BF16),
            pltpu.VMEM((early, early), BF16),
            pltpu.VMEM((early, early), BF16),
            pltpu.VMEM((slots, slots), BF16),
            pltpu.VMEM((slots, slots), BF16),
            pltpu.VMEM((early, early), F32),
            pltpu.VMEM((kraw + 3 * n_col * nd, slots), BF16),
            pltpu.VMEM((kraw, slots), BF16),
            pltpu.VMEM((2, CHUNK, slots), F32),
            pltpu.VMEM((2, slots, CHUNK), BF16),
            pltpu.VMEM((2, slots, CHUNK), BF16),
            dma((3,)),
            dma((n_col, hch)),
            dma((n_col, nch, 2)),
            dma((4, n_col)),
            dma((n_col, hch)),
            dma((3, n_col)),
            dma((n_row, n_col)),
            dma((7, ys * n_col)),
            dma((2,)),
            dma((2,)),
            dma((2,)),
        ],
        compiler_params=pltpu.CompilerParams(
            collective_id=0, has_side_effects=True, vmem_limit_bytes=VMEM_LIMIT
        ),
    )(front, delayed, dest, pivots, flags, diag, off, linv)


def trailing_kernel(c_ref, hi_ref, lo_ref, front_ref, rkeep_ref, ckeep_ref, out_ref, factor_ref):
    columns = c_ref[...]
    factor_ref[...] = columns
    hi, lo = split(columns)
    bh = hi_ref[...]
    acc = mm(hi, bh) + mm(hi, lo_ref[...]) + mm(lo, bh)
    keep = (rkeep_ref[...] > 0.0) & (ckeep_ref[...] > 0.0)
    out_ref[...] = jnp.where(keep, front_ref[...] - acc, 0.0)


def update(columns, side_hi, side_lo, front, row_keep, col_keep):
    rows, cols = front.shape
    slots = columns.shape[1]
    tile = 256
    return pl.pallas_call(
        trailing_kernel,
        grid=(rows // tile,),
        in_specs=[
            pl.BlockSpec((tile, slots), lambda i: (i, 0)),
            pl.BlockSpec((slots, cols), lambda i: (0, 0)),
            pl.BlockSpec((slots, cols), lambda i: (0, 0)),
            pl.BlockSpec((tile, cols), lambda i: (i, 0)),
            pl.BlockSpec((tile, 1), lambda i: (i, 0)),
            pl.BlockSpec((1, cols), lambda i: (0, 0)),
        ],
        out_specs=(
            pl.BlockSpec((tile, cols), lambda i: (i, 0)),
            pl.BlockSpec((tile, slots), lambda i: (i, 0)),
        ),
        out_shape=(
            jax.ShapeDtypeStruct((rows, cols), F32),
            jax.ShapeDtypeStruct((rows, slots), F32),
        ),
        compiler_params=pltpu.CompilerParams(dimension_semantics=("arbitrary",), vmem_limit_bytes=VMEM_LIMIT),
    )(columns, side_hi, side_lo, front, row_keep, col_keep)


def body(front, delayed, dest, pivots, pair_flags, linv, dinv_diag, dinv_off):
    columns, side_hi, side_lo, row_keep, col_keep = gather(
        front, delayed, dest[None, :], pivots[None, :], pair_flags[None, :], dinv_diag[None, :], dinv_off[None, :], linv)
    trailing, factor = update(columns, side_hi, side_lo, front, row_keep, col_keep)
    return (trailing, factor)


def solution(mesh):
    return jax.shard_map(
        body,
        mesh=mesh,
        in_specs=(P("row", "col"), P("col", "row"), P("col"), P(), P(), P(), P(), P()),
        out_specs=(P("row", "col"), P("row", None)),
        check_vma=False,
    )
```
